32 devices in a mesh: sub: 4 (over z), grp: 8 (over y, x, core).
Axes of the slice: x: 2, y: 2, z: 4, core: 2. Of those that a mesh axis runs over, the one named last changes fastest.
Arguments:
- schur: bfloat16 [128, 1024, 1024], P(('sub', 'grp')), as said below
- mortar: bfloat16 [128, 8, 128, 128], P(('sub', 'grp')), may hold values from -0.5 to 0.5
- partner: int32 [128, 4], P(('sub', 'grp')), may hold values from 0 to 15, as said below
- corner_map: int32 [128, 8], P(('sub', 'grp')), may hold values from 0 to 127
- coarse_inv: float32 [4, 128, 128], P('sub'), as said below
- load: float32 [128, 1024, 384], P(('sub', 'grp')), may hold values from -6 to 6
Outputs:
- solution: float32 [128, 1024, 384], P(('sub', 'grp'))
The draws below stay inside these ranges and needn't reach their ends.
Inputs may be any that keep to these rules, and one draw needn't show every extreme that they name: `partner`: within the 4 subdomains of one device, the entries form a permutation of 0 to 15. `schur`: each matrix is symmetric positive definite. `coarse_inv`: each matrix is symmetric positive definite.
All inputs are finite; a program needn't handle non-finite values.
Results may differ from the reference program's by a relative error of at most 0.0025.
Values may be sent and summed in bfloat16 or wider, within the bound.
No kernel may reach another device: no remote copies, remote signals or barrier semaphores. Data moves between devices by JAX's collectives and lax.ppermute only.
A program may use at most 128 MiB of HBM per device.

```python
import math
import jax
import jax.numpy as jnp
from jax import lax

IF = 1024
FB = 128
NF = 8
NCR = 8
NCO = 128
SUBDEV = 4
RHS = 384
ITERS = 2
SUBS = 128
N_SUB = 4
N_GRP = 8


def symmetric_block(key, order, spread, low, high):
    first_key, second_key = jax.random.split(key)
    noise = jax.random.normal(first_key, (order, order), jnp.float32)
    scaled = (noise + noise.T) * (spread / math.sqrt(2.0 * order))
    diagonal = jnp.exp(jax.random.uniform(second_key, (order, 1), jnp.float32, math.log(low), math.log(high)))
    identity = (lax.broadcasted_iota(jnp.int32, (order, order), 0) == lax.broadcasted_iota(jnp.int32, (order, order), 1)).astype(jnp.float32)
    return scaled + identity * diagonal


def draw_schur(key, part):

    def single(index):
        return symmetric_block(jax.random.fold_in(key, index), IF, 0.9, 2.5, 6.0).astype(jnp.bfloat16)
    return lax.map(single, jnp.arange(SUBS, dtype=jnp.int32))


def draw_coarse_inv(key, part):

    def single(index):
        return symmetric_block(jax.random.fold_in(key, index + 7), NCO, 0.4, 1.2, 3.0)
    return lax.map(single, jnp.arange(N_SUB, dtype=jnp.int32))


def draw_partner(key, part):
    device_keys = jax.random.split(jax.random.fold_in(key, 11), SUBS // SUBDEV)
    orders = jax.vmap(lambda single: jax.random.permutation(single, SUBDEV * (NF // 2)))(device_keys)
    return orders.astype(jnp.int32).reshape(SUBS, NF // 2)


def draw_corner_map(key, part):
    mapping = jax.random.randint(jax.random.fold_in(key, 13), (SUBS, NCR), 0, NCO, jnp.int32)
    return mapping.at[0, 0].set(NCO - 1).at[0, 1].set(0)


def block_scale(stream_key, dims, pieces, least, largest):
    level, own = 1.0, jax.random.fold_in(stream_key, 6)
    for position, blocks in pieces:
        draws = jnp.exp(jax.random.uniform(jax.random.fold_in(own, position), (blocks,), jnp.float32, least / len(pieces), largest / len(pieces)))
        level = level * jnp.repeat(draws, dims[position] // blocks).reshape([-1 if axis == position else 1 for axis in range(len(dims))])
    return level


def normal_values(rng, dims, scale, limit, shards=(), held_as=jnp.bfloat16):
    level = block_scale(rng, dims, shards, -0.22, 0.18) if shards else 1.0
    values = jax.random.normal(rng, dims, jnp.float32) * scale * level
    return jnp.minimum(jnp.maximum(values, -limit), limit).astype(held_as)


def setup_inputs(seed: int = 0) -> dict:
    seeds = jax.random.split(jax.random.key(seed), 7)
    schur = draw_schur(jax.random.fold_in(seeds[6], 71), 0)
    mortar = normal_values(seeds[1], (SUBS, NF, FB, FB), FB ** -0.5, 0.5, ((0, 32),))
    partner = draw_partner(jax.random.fold_in(seeds[6], 71), 0)
    corner_map = draw_corner_map(jax.random.fold_in(seeds[6], 71), 0)
    coarse_inv = draw_coarse_inv(jax.random.fold_in(seeds[6], 71), 0)
    load = normal_values(seeds[5], (SUBS, IF, RHS), 1.0, 6.0, ((0, 32),), jnp.float32)
    return dict(schur=schur, mortar=mortar, partner=partner, corner_map=corner_map, coarse_inv=coarse_inv, load=load)


def operate(direction, schur, mortar, mates, inverse, grouped_hot, coarse_inv):
    half_faces = NF // 2
    stride = IF // NCR
    dir_half = direction.astype(jnp.bfloat16)
    stiff = lax.map(lambda couple: jnp.dot(couple[0], couple[1], preferred_element_type=jnp.float32), (schur, dir_half))
    face_rows = dir_half.reshape(SUBS, NF, FB, RHS)
    traces = lax.map(lambda couple: jnp.einsum("fij,fjr->fir", couple[0].astype(jnp.float32), couple[1].astype(jnp.float32)), (mortar, face_rows)).astype(jnp.bfloat16)
    shaped = traces.reshape(N_SUB, N_GRP, SUBDEV, NF, FB, RHS)
    upper = shaped[:, :, :, :half_faces].reshape(N_SUB, N_GRP, SUBDEV * half_faces, FB, RHS)
    lower = shaped[:, :, :, half_faces:].reshape(N_SUB, N_GRP, SUBDEV * half_faces, FB, RHS)
    above = jnp.roll(lower, -1, axis=0)
    upper_mate = jnp.take_along_axis(above, mates[:, :, :, None, None], axis=2)
    reordered = jnp.take_along_axis(upper, inverse[:, :, :, None, None], axis=2)
    lower_mate = jnp.roll(reordered, 1, axis=0)
    jump_upper = (upper.astype(jnp.float32) - upper_mate.astype(jnp.float32)).astype(jnp.bfloat16)
    jump_lower = (lower.astype(jnp.float32) - lower_mate.astype(jnp.float32)).astype(jnp.bfloat16)
    jump_all = jnp.concatenate([jump_upper.reshape(N_SUB, N_GRP, SUBDEV, half_faces, FB, RHS), jump_lower.reshape(N_SUB, N_GRP, SUBDEV, half_faces, FB, RHS)], axis=3).reshape(SUBS, NF, FB, RHS)
    pulled = lax.map(lambda couple: jnp.einsum("fji,fjr->fir", couple[0].astype(jnp.float32), couple[1].astype(jnp.float32)), (mortar, jump_all))
    partial_value = stiff + pulled.reshape(SUBS, IF, RHS)
    corners = direction[:, ::stride, :].reshape(N_SUB, N_GRP * SUBDEV, NCR, RHS)
    coarse_sum = jnp.einsum("nsco,nscr->nor", grouped_hot, corners, precision=lax.Precision.HIGHEST)
    coarse_val = jnp.einsum("nop,npr->nor", coarse_inv, coarse_sum, precision=lax.Precision.HIGHEST)
    corner_add = jnp.einsum("nsco,nor->nscr", grouped_hot, coarse_val, precision=lax.Precision.HIGHEST).reshape(SUBS, NCR, RHS)
    return partial_value.at[:, ::stride, :].add(corner_add)


def reference(schur, mortar, partner, corner_map, coarse_inv, load):
    half_faces = NF // 2
    mates = partner.reshape(N_SUB, N_GRP, SUBDEV * half_faces).astype(jnp.int32)
    inverse = jnp.argsort(mates, axis=-1).astype(jnp.int32)
    onehot = (corner_map[..., None] == jnp.arange(NCO, dtype=jnp.int32)).astype(jnp.float32)
    grouped_hot = onehot.reshape(N_SUB, N_GRP * SUBDEV, NCR, NCO)
    solution = jnp.zeros_like(load)
    residual = load
    direction = load
    norm_now = jnp.sum(residual * residual, axis=(0, 1))
    for step in range(ITERS):
        image = operate(direction, schur, mortar, mates, inverse, grouped_hot, coarse_inv)
        step_len = norm_now / jnp.sum(direction * image, axis=(0, 1))
        solution = solution + step_len * direction
        if step + 1 < ITERS:
            residual = residual - step_len * image
            norm_next = jnp.sum(residual * residual, axis=(0, 1))
            direction = residual + (norm_next / norm_now) * direction
            norm_now = norm_next
    return solution
```

```python
import functools

import jax
import jax.numpy as jnp
from jax import lax
from jax.experimental import pallas as pl
from jax.experimental.pallas import tpu as pltpu
from jax.sharding import PartitionSpec as P

LANES = 128
F32 = jnp.float32
BF16 = jnp.bfloat16


def shifted(block, axis, distance):
    devices = range(lax.axis_size(axis))
    route = [((i - distance) % len(devices), i) for i in devices]
    return lax.ppermute(block, axis, route)


def group_sum(value, axis):
    size = lax.axis_size(axis)
    hop = 1
    while hop < size:
        value = value + lax.ppermute(value, axis, [(i ^ hop, i) for i in range(size)])
        hop *= 2
    return value


def fold_rows(x):
    return jnp.sum(x.reshape(x.shape[0] // 8, 8, x.shape[1]), axis=0)


def smem():
    return pl.BlockSpec(memory_space=pltpu.SMEM)


def whole(shape):
    return pl.BlockSpec(shape, lambda s: (0,) * len(shape))


def first_traces(bounds, partner, cmap, load, mortar, *outs):
    ups, los, norm, csum = outs[: len(bounds)], outs[len(bounds) : 2 * len(bounds)], outs[-2], outs[-1]
    s = pl.program_id(0)
    faces, block = mortar.shape[1], mortar.shape[2]
    half = faces // 2
    corners = cmap.shape[1]
    stride = load.shape[1] // corners

    @pl.when(s == 0)
    def _():
        norm[...] = jnp.zeros_like(norm)
        csum[...] = jnp.zeros_like(csum)

    for f in range(faces):
        rows = load[0, f * block : (f + 1) * block, :]
        norm[...] += fold_rows(rows * rows)
        trace = jnp.dot(mortar[0, f], rows.astype(BF16), preferred_element_type=F32).astype(BF16)
        for (lo, hi), up_ref, lo_ref in zip(bounds, ups, los):
            if f < half:
                up_ref[partner[s, f]] = trace[:, lo:hi]
            else:
                lo_ref[f - half] = trace[:, lo:hi]
    for c in range(corners):
        row = pl.ds(cmap[s, c], 1)
        csum[row, :] += load[0, c * stride : c * stride + 1, :]


def stiff_product(schur, load, out):
    out[0] = jnp.dot(schur[0], load[0].astype(BF16), preferred_element_type=F32)


def first_image(partner, cmap, mortar, stiff, load, up, low, above, below, csum, cinv,
                image, up_out, low_out, jump_out, curv, csum_out, cval):
    s = pl.program_id(0)
    faces, block = mortar.shape[1], mortar.shape[2]
    half = faces // 2
    corners = cmap.shape[1]
    stride = load.shape[1] // corners

    @pl.when(s == 0)
    def _():
        curv[...] = jnp.zeros_like(curv)
        csum_out[...] = jnp.zeros_like(csum_out)
        cval[...] = jnp.dot(cinv[0], csum[...], precision=lax.Precision.HIGHEST, preferred_element_type=F32)

    for f in range(faces):
        if f < half:
            slot = partner[s, f]
            jump = (up[slot].astype(F32) - above[slot].astype(F32)).astype(BF16)
        else:
            jump = (low[f - half].astype(F32) - below[f - half].astype(F32)).astype(BF16)
            jump_out[f - half] = jump
        pulled = lax.dot_general(mortar[0, f], jump, (((0,), (0,)), ((), ())), preferred_element_type=F32)
        rows = slice(f * block, (f + 1) * block)
        image[0, rows, :] = stiff[0, rows, :] + pulled
    for c in range(corners):
        row = pl.ds(cmap[s, c], 1)
        at = slice(c * stride, c * stride + 1)
        value = image[0, at, :] + cval[row, :]
        image[0, at, :] = value
        csum_out[row, :] += value
    for f in range(faces):
        rows = image[0, f * block : (f + 1) * block, :]
        curv[...] += fold_rows(load[0, f * block : (f + 1) * block, :] * rows)
        trace = jnp.dot(mortar[0, f], rows.astype(BF16), preferred_element_type=F32).astype(BF16)
        if f < half:
            up_out[partner[s, f]] = trace
        else:
            low_out[f - half] = trace


def pack_rows(norm, *rest):
    out, curvs = rest[-1], rest[:-1]
    out[...] = jnp.zeros_like(out)
    at = 0
    for ref in (norm,) + curvs:
        for j in range(ref.shape[1] // LANES):
            out[at : at + 1, :] = jnp.sum(ref[:, j * LANES : (j + 1) * LANES], axis=0, keepdims=True)
            at += 1


def step_row(sums, groups, j):
    return sums[j : j + 1, :] / sums[groups + j : groups + j + 1, :]


def residual_sums(bounds, share, sums, schur, load, csum, cinv, *rest):
    count = len(bounds)
    images, csums, norm, energy, resid = rest[:count], rest[count : 2 * count], rest[-3], rest[-2], rest[-1]
    s = pl.program_id(0)
    groups = load.shape[2] // LANES

    def step_of(j):
        return step_row(sums, groups, j)

    @pl.when(s == 0)
    def _():
        norm[...] = jnp.zeros_like(norm)
        for (lo, hi), cs in zip(bounds, csums):
            for j in range(lo // LANES, hi // LANES):
                cols = slice(j * LANES, (j + 1) * LANES)
                own = slice(j * LANES - lo, (j + 1) * LANES - lo)
                coarse = csum[:, cols] - step_of(j) * cs[:, own]
                value = jnp.dot(cinv[0], coarse, precision=lax.Precision.HIGHEST, preferred_element_type=F32)
                energy[:, cols] = share * fold_rows(coarse * value)

    for (lo, hi), image in zip(bounds, images):
        for j in range(lo // LANES, hi // LANES):
            cols = slice(j * LANES, (j + 1) * LANES)
            own = slice(j * LANES - lo, (j + 1) * LANES - lo)
            resid[:, cols] = load[0, :, cols] - step_of(j) * image[0, :, own]
    r = resid[...]
    norm[...] += fold_rows(r * r)
    energy[...] += fold_rows(r * jnp.dot(schur[0], r.astype(BF16), preferred_element_type=F32))


def jump_energy(first, groups, sums, low, recv, jump, out):
    s = pl.program_id(0)

    @pl.when(s == 0)
    def _():
        out[...] = jnp.zeros_like(out)

    for j in range(out.shape[1] // LANES):
        cols = slice(j * LANES, (j + 1) * LANES)
        step = step_row(sums, groups, first + j)
        acc = out[:, cols]
        for k in range(low.shape[0]):
            delta = low[k, :, cols].astype(F32) - recv[k, :, cols].astype(F32)
            value = jump[k, :, cols].astype(F32) - step * delta
            acc += fold_rows(value * value)
        out[:, cols] = acc


def finish(bounds, sums, gathered, load, *rest):
    images, out = rest[:-1], rest[-1]
    groups = load.shape[2] // LANES
    total = jnp.sum(gathered[...], axis=0)
    for (lo, hi), image in zip(bounds, images):
        for j in range(lo // LANES, hi // LANES):
            cols = slice(j * LANES, (j + 1) * LANES)
            own = slice(j * LANES - lo, (j + 1) * LANES - lo)
            norm0 = sums[j : j + 1, :]
            step = step_row(sums, groups, j)
            norm1 = total[j : j + 1, :]
            beta = norm1 / norm0
            curvature = total[groups + j : groups + j + 1, :] - beta * norm1 / step
            step2 = norm1 / curvature
            scale_load = step + step2 * (1.0 + beta)
            scale_image = step2 * step
            out[0, :, cols] = scale_load * load[0, :, cols] - scale_image * image[0, :, own]


def on_device(schur, mortar, partner, corner_map, coarse_inv, load):
    subs, order, columns = load.shape
    faces, block = mortar.shape[1], mortar.shape[2]
    half = faces // 2
    slots = subs * half
    coarse = coarse_inv.shape[1]
    groups = columns // LANES
    cut = columns - LANES if columns > LANES else columns
    bounds = [b for b in ((0, cut), (cut, columns)) if b[1] > b[0]]
    widths = [hi - lo for lo, hi in bounds]
    shape = jax.ShapeDtypeStruct
    params = pltpu.CompilerParams(dimension_semantics=("arbitrary",))

    per_sub = lambda width, at: pl.BlockSpec((1, order, width), lambda s: (s, 0, at))
    mortar_spec = pl.BlockSpec((1, faces, block, block), lambda s: (s, 0, 0, 0))
    schur_spec = pl.BlockSpec((1, order, order), lambda s: (s, 0, 0))
    slot_spec = lambda width: pl.BlockSpec((half, block, width), lambda s: (s, 0, 0))
    faces_of = lambda width: shape((slots, block, width), BF16)
    cinv_spec = whole((1, coarse, coarse))

    first = pl.pallas_call(
        functools.partial(first_traces, bounds),
        grid=(subs,),
        in_specs=[smem(), smem(), per_sub(columns, 0), mortar_spec],
        out_specs=[whole((slots, block, w)) for w in widths]
        + [slot_spec(w) for w in widths]
        + [whole((8, columns)), whole((coarse, columns))],
        out_shape=[faces_of(w) for w in widths] * 2 + [shape((8, columns), F32), shape((coarse, columns), F32)],
        compiler_params=params,
        name="first_traces",
    )(partner, corner_map, load, mortar)
    ups, lows = first[: len(bounds)], first[len(bounds) : 2 * len(bounds)]
    norm_part, csum_part = first[-2], first[-1]

    belows = []
    aboves = []
    for k in range(len(bounds)):
        belows.append(shifted(ups[k], "sub", 1))
        aboves.append(shifted(lows[k], "sub", -1))
    csum = group_sum(csum_part, "grp")

    stiff = pl.pallas_call(
        stiff_product,
        grid=(subs,),
        in_specs=[schur_spec, per_sub(columns, 0)],
        out_specs=per_sub(columns, 0),
        out_shape=shape((subs, order, columns), F32),
        compiler_params=params,
        name="stiff_product",
    )(schur, load)

    images, jumps, low2s, up2s, curvs, csum2s = [], [], [], [], [], []
    for k, (lo, hi) in enumerate(bounds):
        w = hi - lo
        outs = pl.pallas_call(
            first_image,
            grid=(subs,),
            in_specs=[
                smem(), smem(), mortar_spec, per_sub(w, lo // w), per_sub(w, lo // w),
                whole((slots, block, w)), slot_spec(w), whole((slots, block, w)), slot_spec(w),
                pl.BlockSpec((coarse, w), lambda s, at=lo // w: (0, at)), cinv_spec,
            ],
            out_specs=[per_sub(w, 0), whole((slots, block, w)), slot_spec(w), slot_spec(w),
                       whole((8, w)), whole((coarse, w))],
            out_shape=[shape((subs, order, w), F32), faces_of(w), faces_of(w), faces_of(w),
                       shape((8, w), F32), shape((coarse, w), F32)],
            scratch_shapes=[pltpu.VMEM((coarse, w), F32)],
            compiler_params=params,
            name=f"first_image_{k}",
        )(partner, corner_map, mortar, stiff, load, ups[k], lows[k], aboves[k], belows[k], csum, coarse_inv)
        images.append(outs[0])
        up2s.append(outs[1])
        low2s.append(outs[2])
        jumps.append(outs[3])
        curvs.append(outs[4])
        csum2s.append(group_sum(outs[5], "grp"))

    pack = lambda *parts: pl.pallas_call(
        pack_rows, out_shape=shape((8, LANES), F32), name="pack_rows"
    )(*parts)

    part = group_sum(pack(norm_part, *curvs), "grp")
    recvs = [shifted(up2s[k], "sub", 1) for k in range(len(bounds))]
    sums = part
    for d in range(1, lax.axis_size("sub")):
        sums = sums + shifted(part, "sub", d)

    share = 1.0 / lax.axis_size("grp")
    sums_spec = whole((8, LANES))
    norm1, energy = pl.pallas_call(
        functools.partial(residual_sums, bounds, share),
        grid=(subs,),
        in_specs=[sums_spec, schur_spec, per_sub(columns, 0), whole((coarse, columns)), cinv_spec]
        + [per_sub(w, 0) for w in widths]
        + [whole((coarse, w)) for w in widths],
        out_specs=[whole((8, columns)), whole((8, columns))],
        out_shape=[shape((8, columns), F32)] * 2,
        scratch_shapes=[pltpu.VMEM((order, columns), F32)],
        compiler_params=params,
        name="residual_sums",
    )(sums, schur, load, csum, coarse_inv, *images, *csum2s)

    energies = []
    for k, (lo, hi) in enumerate(bounds):
        w = hi - lo
        energies.append(pl.pallas_call(
            functools.partial(jump_energy, lo // LANES, groups),
            grid=(subs,),
            in_specs=[sums_spec, slot_spec(w), slot_spec(w), slot_spec(w)],
            out_specs=whole((8, w)),
            out_shape=shape((8, w), F32),
            compiler_params=params,
            name=f"jump_energy_{k}",
        )(sums, low2s[k], recvs[k], jumps[k]))

    packed = pack(norm1, energy + jnp.concatenate(energies, axis=1))
    devices = lax.axis_size("sub") * lax.axis_size("grp")
    spread = jnp.broadcast_to(packed[None], (devices,) + packed.shape)
    gathered = lax.all_to_all(spread, ("sub", "grp"), 0, 0, tiled=True)

    return pl.pallas_call(
        functools.partial(finish, bounds),
        grid=(subs,),
        in_specs=[sums_spec, whole((devices, 8, LANES)), per_sub(columns, 0)] + [per_sub(w, 0) for w in widths],
        out_specs=per_sub(columns, 0),
        out_shape=shape((subs, order, columns), F32),
        compiler_params=params,
        name="finish",
    )(sums, gathered, load, *images)


def solution(mesh):
    return jax.shard_map(
        on_device,
        mesh=mesh,
        in_specs=(
            P(("sub", "grp"), None, None),
            P(("sub", "grp"), None, None, None),
            P(("sub", "grp"), None),
            P(("sub", "grp"), None),
            P("sub", None, None),
            P(("sub", "grp"), None, None),
        ),
        out_specs=P(("sub", "grp"), None, None),
        check_vma=False,
    )
```

```python
import functools

import jax
import jax.numpy as jnp
from jax import lax
from jax.experimental import pallas as pl
from jax.experimental.pallas import tpu as pltpu
from jax.sharding import PartitionSpec as P


LANES = 128
F32 = jnp.float32
BF16 = jnp.bfloat16


def shifted(block, axis, distance):
    devices = range(lax.axis_size(axis))
    route = [((i - distance) % len(devices), i) for i in devices]
    return lax.ppermute(block, axis, route)


def group_sum(value, axis):
    size = lax.axis_size(axis)
    hop = 1
    while hop < size:
        value = value + lax.ppermute(value, axis, [(i ^ hop, i) for i in range(size)])
        hop *= 2
    return value


def hub_sum(value, axis):
    size = lax.axis_size(axis)
    hub = size - 1
    total = value
    for i in range(hub):
        total = total + lax.ppermute(value, axis, [(i, hub)])
    others = [lax.ppermute(total, axis, [(hub, i)]) for i in range(hub)]
    return [total] + others


def fold_rows(x):
    return jnp.sum(x.reshape(x.shape[0] // 8, 8, x.shape[1]), axis=0)


def vmem(x):
    return pltpu.with_memory_space_constraint(x, pltpu.VMEM)


def hbm(x):
    return pltpu.with_memory_space_constraint(x, pltpu.HBM)


VMEM = pl.BlockSpec(memory_space=pltpu.VMEM)
ANY = pl.BlockSpec(memory_space=pl.ANY)


def row_sum(x):
    return jnp.sum(x, axis=0, keepdims=True)


def group_cols(j):
    return slice(j * LANES, (j + 1) * LANES)


def fetch_tables(partner_hbm, cmap_hbm, partner, cmap, sems):
    return [
        pltpu.make_async_copy(partner_hbm, partner, sems.at[0]),
        pltpu.make_async_copy(cmap_hbm, cmap, sems.at[1]),
    ]


def first_traces(lo, copies, partner_hbm, cmap_hbm, load_hbm, mortar_in, *refs):
    if copies:
        load, mortar, up, low, norm, csum, partner, cmap, sems = refs
    else:
        load, up, low, norm, csum, partner, cmap, sems = refs
        mortar = mortar_in
    subs, order, width = load.shape
    faces, block = mortar.shape[1], mortar.shape[2]
    half = faces // 2
    corners = cmap.shape[1]
    stride = order // corners

    def fetch(s):
        moves = [pltpu.make_async_copy(load_hbm.at[s, :, pl.ds(lo, width)], load.at[s], sems.at[0, s])]
        if copies:
            moves.append(pltpu.make_async_copy(mortar_in.at[s], mortar.at[s], sems.at[1, s]))
        return moves

    tables = fetch_tables(partner_hbm, cmap_hbm, partner, cmap, sems.at[2])
    for move in tables:
        move.start()
    for s in range(subs):
        for move in fetch(s):
            move.start()
    norm[...] = jnp.zeros_like(norm)
    csum[...] = jnp.zeros_like(csum)
    for move in tables:
        move.wait()
    for s in range(subs):
        for move in fetch(s):
            move.wait()
        for f in range(faces):
            rows = load[s, f * block : (f + 1) * block, :]
            norm[...] += fold_rows(rows * rows)
            trace = jnp.dot(mortar[s, f], rows.astype(BF16), preferred_element_type=F32).astype(BF16)
            if f < half:
                up[partner[s, f]] = trace
            else:
                low[s * half + f - half] = trace
        for c in range(corners):
            row = pl.ds(cmap[s, c], 1)
            csum[row, :] += load[s, c * stride : c * stride + 1, :]


def stiff_product(schur_hbm, mortar, *refs):
    loads, (out_a, out_b, schur, flipped, sems) = refs[:-5], refs[-5:]
    subs = schur.shape[0]

    def fetch(s):
        return pltpu.make_async_copy(schur_hbm.at[s], schur.at[s], sems.at[s])

    for s in range(subs):
        fetch(s).start()

    def work(s, _):
        fetch(s).wait()
        value = jnp.concatenate([load[s].astype(BF16) for load in loads], axis=1)
        product = jnp.dot(schur[s], value, preferred_element_type=F32)
        out_a[s] = product[:, : out_a.shape[2]]
        out_b[s] = product[:, out_a.shape[2] :]
        for f in range(mortar.shape[1]):
            flipped[s, f] = mortar[s, f].T
        return 0

    lax.fori_loop(0, subs, work, 0)


def first_image(lo, pieces, groups, share, partner_hbm, cmap_hbm, mortar, flipped, stiff, csum, cinv, *refs):
    ins, earlier, refs = refs[: 6 * pieces], refs[6 * pieces], refs[6 * pieces + 1 :]
    loads, norms, ups, lows, aboves, belows = (ins[i * pieces : (i + 1) * pieces] for i in range(6))
    up_cuts, refs = refs[1:-8], refs[:1] + refs[-8:]
    image, low_out, jump_out, sums, cval, up_out, partner, cmap, sems = refs
    subs, order, width = image.shape
    faces, block = mortar.shape[1], mortar.shape[2]
    half = faces // 2
    corners = cmap.shape[1]
    coarse = csum.shape[0]
    stride = order // corners
    cols = slice(lo, lo + width)
    tables = fetch_tables(partner_hbm, cmap_hbm, partner, cmap, sems)
    for move in tables:
        move.start()
    sums[...] = jnp.zeros_like(sums)
    cval[...] = jnp.dot(cinv[0], csum[:, cols], precision=lax.Precision.HIGHEST, preferred_element_type=F32)
    for move in tables:
        move.wait()

    def difference(own, other, slot):
        return jnp.concatenate(
            [(a[slot].astype(F32) - b[slot].astype(F32)).astype(BF16) for a, b in zip(own, other)], axis=1
        )

    def work(s, curv):
        for f in range(faces):
            if f < half:
                jump = difference(ups, aboves, partner[s, f])
            else:
                jump = difference(lows, belows, s * half + f - half)
                jump_out[s * half + f - half] = jump
            pulled = jnp.dot(flipped[s, f], jump, preferred_element_type=F32)
            rows = slice(f * block, (f + 1) * block)
            image[s, rows, :] = stiff[s, rows, :] + pulled
        for c in range(corners):
            row = pl.ds(cmap[s, c], 1)
            at = slice(c * stride, c * stride + 1)
            value = image[s, at, :] + cval[row, :]
            image[s, at, :] = value
            sums[row, :] += value
        for f in range(faces):
            at = slice(f * block, (f + 1) * block)
            rows = image[s, at, :]
            curv = tuple(
                acc + fold_rows(load[s, at, :] * rows[:, group_cols(j)])
                for j, (acc, load) in enumerate(zip(curv, loads))
            )
            trace = jnp.dot(mortar[s, f], rows.astype(BF16), preferred_element_type=F32).astype(BF16)
            if f < half:
                up_out[partner[s, f]] = trace
            else:
                low_out[s * half + f - half] = trace
        return curv

    curv = lax.fori_loop(0, subs, work, tuple(jnp.zeros((8, LANES), F32) for _ in loads))
    at = 0
    for cut in up_cuts:
        cut[...] = up_out[at : at + cut.shape[0]]
        at += cut.shape[0]
    first = lo // LANES
    for j in range(pieces):
        for row, value in ((first + j, norms[j][...]), (groups + first + j, curv[j])):
            sums[coarse + row : coarse + row + 1, :LANES] = row_sum(value)
    for j in range(first):
        for row in (j, groups + j):
            at = slice(coarse + row, coarse + row + 1)
            sums[at, :] = share * earlier[at, :LANES]


def residual_sums(share, hops, groups, *refs):
    parts, refs = refs[:hops], refs[hops:]
    schur, csum, cinv, csum_a, csum_b, image_a, image_b = refs[:7]
    loads, (total, norm, energy, resid) = refs[7 : 7 + groups], refs[7 + groups :]
    coarse = csum.shape[0]
    value = jnp.where(lax.axis_index("sub") == hops - 1, parts[0][...], 0.0)
    for ref in parts[1:]:
        value += ref[...]
    for j in range(groups):
        total[0:1, group_cols(j)] = value[j : j + 1, :]
        total[1:2, group_cols(j)] = value[groups + j : groups + j + 1, :]
    step = total[0:1, :] / total[1:2, :]
    inner = jnp.concatenate([csum_a[:coarse, :], csum_b[:coarse, :]], axis=1)
    change = csum[...] - step * inner
    field = jnp.dot(cinv[0], change, precision=lax.Precision.HIGHEST, preferred_element_type=F32)
    norm[...] = jnp.zeros_like(norm)
    energy[...] = share * fold_rows(change * field)

    def work(s, _):
        for j, load in enumerate(loads):
            cols = group_cols(j)
            image, own = (image_a, cols) if j + 1 < groups else (image_b, group_cols(0))
            resid[:, cols] = load[s] - step[:, cols] * image[s, :, own]
        r = resid[...]
        norm[...] += fold_rows(r * r)
        energy[...] += fold_rows(r * jnp.dot(schur[s], r.astype(BF16), preferred_element_type=F32))
        return 0

    lax.fori_loop(0, schur.shape[0], work, 0)


def jump_squares(step, low, jump, recvs, cols):
    start, acc = 0, jnp.zeros((8, LANES), F32)
    for recv in recvs:

        def one(k, acc, recv=recv, start=start):
            delta = low[start + k, :, cols].astype(F32) - recv[k, :, cols].astype(F32)
            value = jump[start + k, :, cols].astype(F32) - step * delta
            return acc + fold_rows(value * value)

        acc = lax.fori_loop(0, recv.shape[0], one, acc, unroll=2)
        start += recv.shape[0]
    return acc


def add_jumps(total, energy, low, jump, *refs):
    recvs, out = refs[:-1], refs[-1]
    wide = low.shape[2]
    out[:, wide:] = energy[:, wide:]
    for j in range(wide // LANES):
        cols = group_cols(j)
        step = total[0:1, cols] / total[1:2, cols]
        out[:, cols] = energy[:, cols] + jump_squares(step, low, jump, recvs, cols)


def last_sums(total, norm, energy, low, jump, *refs):
    recvs, out = refs[:-1], refs[-1]
    groups = norm.shape[1] // LANES
    last = group_cols(groups - 1)
    rows = [row_sum(norm[:, group_cols(j)]) for j in range(groups)]
    rows += [row_sum(energy[:, group_cols(j)]) for j in range(groups - 1)]
    step = total[0:1, last] / total[1:2, last]
    rows.append(row_sum(energy[:, last] + jump_squares(step, low, jump, recvs, group_cols(0))))
    rows.append(jnp.zeros((8 - len(rows), LANES), F32))
    out[...] = jnp.broadcast_to(jnp.concatenate(rows, axis=0)[None], out.shape)


def finish(total, gathered, *refs):
    loads, (image_a, image_b, out_hbm, stage, sems) = refs[:-5], refs[-5:]
    groups = len(loads)
    subs = stage.shape[0]
    second = jnp.sum(gathered[...], axis=0)

    def send(s):
        return pltpu.make_async_copy(stage.at[s], out_hbm.at[s], sems.at[s])

    scales = []
    for j in range(groups):
        norm0 = total[0:1, group_cols(j)]
        step = norm0 / total[1:2, group_cols(j)]
        norm1 = second[j : j + 1, :]
        beta = norm1 / norm0
        step2 = norm1 / (second[groups + j : groups + j + 1, :] - beta * norm1 / step)
        scales.append((step + step2 * (1.0 + beta), step2 * step))
    for s in range(subs):
        for j in range(groups):
            image, cols = (image_a, group_cols(j)) if j + 1 < groups else (image_b, group_cols(0))
            stage[s, :, group_cols(j)] = scales[j][0] * loads[j][s] - scales[j][1] * image[s, :, cols]
        send(s).start()
    for s in range(subs):
        send(s).wait()


def call(kernel, in_specs, outs, scratch=(), limit=5, in_hbm=(), alias=None):
    return pl.pallas_call(
        kernel,
        in_specs=in_specs,
        out_specs=[ANY if i in in_hbm else VMEM for i in range(len(outs))],
        out_shape=outs,
        scratch_shapes=list(scratch),
        input_output_aliases=alias or {},
        compiler_params=pltpu.CompilerParams(vmem_limit_bytes=limit * 2**20),
    )


def iterate(schur, mortar, partner, corner_map, coarse_inv, load):
    subs, order, columns = load.shape
    faces, block = mortar.shape[1], mortar.shape[2]
    half = faces // 2
    slots = subs * half
    coarse = coarse_inv.shape[1]
    groups = columns // LANES
    dma = pltpu.SemaphoreType.DMA
    table_scratch = [pltpu.SMEM(partner.shape, partner.dtype), pltpu.SMEM(corner_map.shape, corner_map.dtype)]
    tables = (hbm(partner), hbm(corner_map))

    def traces_of(width):
        return pltpu.VMEM((slots, block, width), BF16)

    loads, norms, ups, lows, csums, aboves, belows = [], [], [], [], [], [], []
    held_mortar = hbm(mortar)
    for j in range(groups):
        outs = [pltpu.VMEM((subs, order, LANES), F32)]
        if j == 0:
            outs.append(pltpu.VMEM(mortar.shape, BF16))
        outs += [traces_of(LANES)] * 2 + [pltpu.VMEM((8, LANES), F32), pltpu.VMEM((coarse, LANES), F32)]
        got = list(call(
            functools.partial(first_traces, j * LANES, j == 0),
            [ANY, ANY, ANY, ANY if j == 0 else VMEM], outs, table_scratch + [dma((3, max(subs, 2)))],
        )(*tables, hbm(load), held_mortar))
        loads.append(vmem(got.pop(0)))
        if j == 0:
            held_mortar = vmem(got.pop(0))
        belows.append(vmem(shifted(got[0], "sub", 1)))
        aboves.append(vmem(shifted(got[1], "sub", -1)))
        ups.append(vmem(got[0]))
        lows.append(vmem(got[1]))
        norms.append(vmem(got[2]))
        csums.append(got[3])
    csum = vmem(group_sum(jnp.concatenate(csums, axis=1), "grp"))

    *stiff, held_schur, flipped = call(
        stiff_product, [ANY] + [VMEM] * (1 + groups),
        [pltpu.VMEM((subs, order, w), F32) for w in (columns - LANES, LANES)]
        + [pltpu.VMEM(schur.shape, BF16), pltpu.VMEM(mortar.shape, BF16)], [dma((subs,))],
    )(hbm(schur), held_mortar, *loads)
    held_schur, flipped = vmem(held_schur), vmem(flipped)

    bounds = ((0, groups - 1), (groups - 1, groups))
    share = 1.0 / lax.axis_size("grp")
    images, jumps, low2s, recvs, csum2s = [], [], [], [], []
    cuts = ((slots - slots // 8, slots // 8), (5 * slots // 16, slots - 5 * slots // 16))
    for k, (lo, hi) in enumerate(bounds):
        n, w = hi - lo, (hi - lo) * LANES
        pick = [x[lo:hi] for x in (loads, norms, ups, lows, aboves, belows)]
        got = call(
            functools.partial(first_image, lo * LANES, n, groups, share),
            [ANY, ANY] + [VMEM] * (6 + 6 * n),
            [pltpu.VMEM((subs, order, w), F32)]
            + [pltpu.VMEM((size, block, w), BF16) for size in cuts[k]]
            + [traces_of(w)] * 2 + [pltpu.VMEM((coarse + 8, w), F32)],
            [pltpu.VMEM((coarse, w), F32), traces_of(w)] + table_scratch + [dma((2,))], alias={4: 0},
        )(*tables, held_mortar, flipped, vmem(stiff[k]), csum, coarse_inv, *sum(pick, []), csum2s[0] if k else csum)
        image, *up2, low2, jump, sums = got
        images.append(vmem(image))
        low2s.append(vmem(low2))
        jumps.append(vmem(jump))
        sums = group_sum(sums, "grp")
        if not k:
            csum, sums = lax.optimization_barrier((csum, sums))
            csum = vmem(csum)
        csum2s.append(vmem(sums))
        recvs.append([])
        for piece in up2:
            recvs[-1].append(vmem(shifted(piece, "sub", 1)))

    totals = [vmem(x) for x in hub_sum(sums[coarse:], "sub")]
    hops = len(totals)
    total, norm1, energy = call(
        functools.partial(residual_sums, share, hops, groups),
        [VMEM] * (hops + 7 + groups), [pltpu.VMEM((8, columns), F32)] * 3, [pltpu.VMEM((order, columns), F32)],
    )(*totals, held_schur, csum, coarse_inv, *csum2s, *images, *loads)
    total, norm1 = vmem(total), vmem(norm1)
    energy = vmem(call(
        add_jumps, [VMEM] * (4 + len(recvs[0])), [pltpu.VMEM(energy.shape, F32)],
    )(total, vmem(energy), low2s[0], jumps[0], *recvs[0])[0])

    devices = lax.axis_size("sub") * lax.axis_size("grp")
    spread = call(
        last_sums, [VMEM] * (5 + len(recvs[1])), [pltpu.VMEM((devices, 8, LANES), F32)],
    )(total, norm1, energy, low2s[1], jumps[1], *recvs[1])[0]
    gathered = lax.all_to_all(spread, ("sub", "grp"), 0, 0, tiled=True)

    return call(
        finish, [VMEM] * (4 + groups),
        [jax.ShapeDtypeStruct((subs, order, columns), F32)],
        [pltpu.VMEM((subs, order, columns), F32), dma((subs,))], limit=9, in_hbm=(0,),
    )(total, vmem(gathered), *loads, *images)[0]


def solution(mesh):
    return jax.shard_map(
        iterate,
        mesh=mesh,
        in_specs=(
            P(("sub", "grp"), None, None),
            P(("sub", "grp"), None, None, None),
            P(("sub", "grp"), None),
            P(("sub", "grp"), None),
            P("sub", None, None),
            P(("sub", "grp"), None, None),
        ),
        out_specs=P(("sub", "grp"), None, None),
        check_vma=False,
    )
```

```python
import functools

import jax
import jax.numpy as jnp
from jax import lax
from jax.experimental import pallas as pl
from jax.experimental.pallas import tpu as pltpu
from jax.sharding import PartitionSpec as P


LANES = 128
F32 = jnp.float32
BF16 = jnp.bfloat16


def shifted(block, axis, distance):
    devices = range(lax.axis_size(axis))
    route = [((i - distance) % len(devices), i) for i in devices]
    return lax.ppermute(block, axis, route)


def group_sum(value, axis):
    size = lax.axis_size(axis)
    hop = 1
    while hop < size:
        value = value + lax.ppermute(value, axis, [(i ^ hop, i) for i in range(size)])
        hop *= 2
    return value


def hub_sum(value, axis):
    size = lax.axis_size(axis)
    hub = size - 1
    total = value
    for d in range(hub, 0, -1):
        route = [(i, (i + d) % size) for i in range(size) if (i + d) % size >= hub - 1]
        total = total + lax.ppermute(value, axis, route)
    others = [lax.ppermute(total, axis, [(hub, i)]) for i in range(hub - 1)]
    return [total] + others


def fold_rows(x):
    return jnp.sum(x.reshape(x.shape[0] // 8, 8, x.shape[1]), axis=0)


def vmem(x):
    return pltpu.with_memory_space_constraint(x, pltpu.VMEM)


def hbm(x):
    return pltpu.with_memory_space_constraint(x, pltpu.HBM)


VMEM = pl.BlockSpec(memory_space=pltpu.VMEM)
ANY = pl.BlockSpec(memory_space=pl.ANY)


def row_sum(x):
    return jnp.sum(x, axis=0, keepdims=True)


def group_cols(j):
    return slice(j * LANES, (j + 1) * LANES)


def fetch_tables(partner_hbm, cmap_hbm, partner, cmap, sems):
    return [
        pltpu.make_async_copy(partner_hbm, partner, sems.at[0]),
        pltpu.make_async_copy(cmap_hbm, cmap, sems.at[1]),
    ]


def lead_traces(load_hbm, mortar_hbm, low, load, mortar, sems):
    subs, half, block = mortar.shape[:3]
    width = load.shape[2]

    def fetch(s):
        rows = pl.ds(half * block, half * block)
        return [
            pltpu.make_async_copy(load_hbm.at[s, rows, pl.ds(0, width)], load.at[s], sems.at[0, s]),
            pltpu.make_async_copy(mortar_hbm.at[s, pl.ds(half, half)], mortar.at[s], sems.at[1, s]),
        ]

    for s in range(subs):
        for move in fetch(s):
            move.start()
    for s in range(subs):
        for move in fetch(s):
            move.wait()
        for f in range(half):
            rows = load[s, f * block : (f + 1) * block, :].astype(BF16)
            low[s * half + f] = jnp.dot(mortar[s, f], rows, preferred_element_type=F32).astype(BF16)


def first_traces(lo, copies, partner_hbm, cmap_hbm, load_hbm, mortar_in, *refs):
    if copies:
        load, mortar, up, norm, csum, partner, cmap, sems = refs
    else:
        load, up, low, norm, csum, partner, cmap, sems = refs
        mortar = mortar_in
    subs, order, width = load.shape
    faces, block = mortar.shape[1], mortar.shape[2]
    half = faces // 2
    corners = cmap.shape[1]
    stride = order // corners

    def fetch(s):
        moves = [pltpu.make_async_copy(load_hbm.at[s, :, pl.ds(lo, width)], load.at[s], sems.at[0, s])]
        if copies:
            moves.append(pltpu.make_async_copy(mortar_in.at[s], mortar.at[s], sems.at[1, s]))
        return moves

    tables = fetch_tables(partner_hbm, cmap_hbm, partner, cmap, sems.at[2])
    for move in tables:
        move.start()
    for s in range(subs):
        for move in fetch(s):
            move.start()
    norm[...] = jnp.zeros_like(norm)
    csum[...] = jnp.zeros_like(csum)
    for move in tables:
        move.wait()
    for s in range(subs):
        for move in fetch(s):
            move.wait()
        for f in range(faces):
            rows = load[s, f * block : (f + 1) * block, :]
            norm[...] += fold_rows(rows * rows)
            if copies and f >= half:
                continue
            trace = jnp.dot(mortar[s, f], rows.astype(BF16), preferred_element_type=F32).astype(BF16)
            if f < half:
                up[partner[s, f]] = trace
            else:
                low[s * half + f - half] = trace
        for c in range(corners):
            row = pl.ds(cmap[s, c], 1)
            csum[row, :] += load[s, c * stride : c * stride + 1, :]


def stiff_product(schur_hbm, mortar, *refs):
    loads, (out_a, out_b, schur, flipped, sems) = refs[:-5], refs[-5:]
    subs = schur.shape[0]

    def fetch(s):
        return pltpu.make_async_copy(schur_hbm.at[s], schur.at[s], sems.at[s])

    for s in range(subs):
        fetch(s).start()

    def work(s, _):
        fetch(s).wait()
        value = jnp.concatenate([load[s].astype(BF16) for load in loads], axis=1)
        product = jnp.dot(schur[s], value, preferred_element_type=F32)
        out_a[s] = product[:, : out_a.shape[2]]
        out_b[s] = product[:, out_a.shape[2] :]
        for f in range(mortar.shape[1]):
            flipped[s, f] = mortar[s, f].T
        return 0

    lax.fori_loop(0, subs, work, 0)


def first_image(lo, pieces, groups, share, partner_hbm, cmap_hbm, mortar, flipped, stiff, csum, cinv, *refs):
    ins, earlier, refs = refs[: 6 * pieces], refs[6 * pieces], refs[6 * pieces + 1 :]
    loads, norms, ups, lows, aboves, belows = (ins[i * pieces : (i + 1) * pieces] for i in range(6))
    tail_in, (send, rest), refs = refs[:-11], refs[-10:-8], refs[-11:-10] + refs[-8:]
    image, low_out, jump_out, sums, cval, up_out, partner, cmap, sems = refs
    subs, order, width = image.shape
    faces, block = mortar.shape[1], mortar.shape[2]
    half = faces // 2
    corners = cmap.shape[1]
    coarse = csum.shape[0]
    stride = order // corners
    cols = slice(lo, lo + width)
    tables = fetch_tables(partner_hbm, cmap_hbm, partner, cmap, sems)
    for move in tables:
        move.start()
    sums[...] = jnp.zeros_like(sums)
    cval[...] = jnp.dot(cinv[0], csum[:, cols], precision=lax.Precision.HIGHEST, preferred_element_type=F32)
    for move in tables:
        move.wait()

    def difference(own, other, slot):
        return jnp.concatenate(
            [(a[slot].astype(F32) - b[slot].astype(F32)).astype(BF16) for a, b in zip(own, other)], axis=1
        )

    def work(s, curv):
        for f in range(faces):
            if f < half:
                jump = difference(ups, aboves, partner[s, f])
            else:
                jump = difference(lows, belows, s * half + f - half)
                jump_out[s * half + f - half] = jump
            pulled = jnp.dot(flipped[s, f], jump, preferred_element_type=F32)
            rows = slice(f * block, (f + 1) * block)
            image[s, rows, :] = stiff[s, rows, :] + pulled
        for c in range(corners):
            row = pl.ds(cmap[s, c], 1)
            at = slice(c * stride, c * stride + 1)
            value = image[s, at, :] + cval[row, :]
            image[s, at, :] = value
            sums[row, :] += value
        for f in range(faces):
            at = slice(f * block, (f + 1) * block)
            rows = image[s, at, :]
            curv = tuple(
                acc + fold_rows(load[s, at, :] * rows[:, group_cols(j)])
                for j, (acc, load) in enumerate(zip(curv, loads))
            )
            trace = jnp.dot(mortar[s, f], rows.astype(BF16), preferred_element_type=F32).astype(BF16)
            if f < half:
                up_out[partner[s, f]] = trace
            else:
                low_out[s * half + f - half] = trace
        return curv

    curv = lax.fori_loop(0, subs, work, tuple(jnp.zeros((8, LANES), F32) for _ in loads))
    first = lo // LANES
    if first:
        kept = first * tail_in[0].shape[0]
        for at in range(kept):
            send[at] = tail_in[0][at // first, :, group_cols(at % first)]
        send[kept:] = up_out[: send.shape[0] - kept]
    else:
        send[...] = up_out[: send.shape[0]]
    rest[...] = up_out[up_out.shape[0] - rest.shape[0] :]
    for j in range(pieces):
        for row, value in ((first + j, norms[j][...]), (groups + first + j, curv[j])):
            sums[coarse + row : coarse + row + 1, :LANES] = row_sum(value)
    for j in range(first):
        for row in (j, groups + j):
            at = slice(coarse + row, coarse + row + 1)
            sums[at, :] = share * earlier[at, :LANES]


def residual_sums(share, hops, groups, *refs):
    parts, refs = refs[:hops], refs[hops:]
    schur, csum, cinv, csum_a, csum_b, image_a, image_b = refs[:7]
    loads, (low, jump), refs = refs[7 : 7 + groups], refs[7 + groups : 9 + groups], refs[9 + groups :]
    recvs, (total, norm, energy, resid) = refs[:-4], refs[-4:]
    coarse = csum.shape[0]
    value = jnp.where(lax.axis_index("sub") + 1 >= hops, parts[0][...], 0.0)
    for ref in parts[1:]:
        value += ref[...]
    for j in range(groups):
        total[0:1, group_cols(j)] = value[j : j + 1, :]
        total[1:2, group_cols(j)] = value[groups + j : groups + j + 1, :]
    step = total[0:1, :] / total[1:2, :]
    inner = jnp.concatenate([csum_a[:coarse, :], csum_b[:coarse, :]], axis=1)
    change = csum[...] - step * inner
    field = jnp.dot(cinv[0], change, precision=lax.Precision.HIGHEST, preferred_element_type=F32)
    norm[...] = jnp.zeros_like(norm)
    energy[...] = share * fold_rows(change * field)

    slots, subs = low.shape[0], schur.shape[0]

    def received(k, j):
        whole, mixed = recvs
        if k < whole.shape[0]:
            return whole[k, :, group_cols(j)]
        return mixed[(k - whole.shape[0]) * (groups - 1) + j]

    for s in range(subs):
        for j, load in enumerate(loads):
            cols = group_cols(j)
            image, own = (image_a, cols) if j + 1 < groups else (image_b, group_cols(0))
            resid[:, cols] = load[s] - step[:, cols] * image[s, :, own]
        r = resid[...]
        norm[...] += fold_rows(r * r)
        energy[...] += fold_rows(r * jnp.dot(schur[s], r.astype(BF16), preferred_element_type=F32))
        for j in range(groups - 1):
            cols = group_cols(j)
            acc = energy[:, cols]
            for k in range(s * slots // subs, (s + 1) * slots // subs):
                delta = low[k, :, cols].astype(F32) - received(k, j).astype(F32)
                value = jump[k, :, cols].astype(F32) - step[:, cols] * delta
                acc += fold_rows(value * value)
            energy[:, cols] = acc


def jump_squares(step, low, jump, recvs, cols):
    acc, start = jnp.zeros((8, LANES), F32), low.shape[0] - sum(recv.shape[0] for recv in recvs)
    for recv in recvs:

        def one(k, acc, recv=recv, start=start):
            delta = low[start + k, :, cols].astype(F32) - recv[k, :, cols].astype(F32)
            value = jump[start + k, :, cols].astype(F32) - step * delta
            return acc + fold_rows(value * value)

        acc = lax.fori_loop(max(-start, 0), recv.shape[0], one, acc, unroll=2)
        start += recv.shape[0]
    return acc


def last_sums(total, norm, energy, low, jump, *refs):
    recvs, out = refs[:-1], refs[-1]
    groups = norm.shape[1] // LANES
    last = group_cols(groups - 1)
    step = total[0:1, last] / total[1:2, last]
    ending = row_sum(energy[:, last] + jump_squares(step, low, jump, recvs, group_cols(0)))
    for d in range(out.shape[0]):
        out[d, 0:1, :] = row_sum(norm[...])
        out[d, 1:2, :] = row_sum(energy[...])
        out[d, 1:2, last] = ending


def finish(total, gathered, *refs):
    loads, (image_a, image_b, out_hbm, stage, sems) = refs[:-5], refs[-5:]
    groups = len(loads)
    subs = stage.shape[0]
    second = jnp.sum(gathered[...], axis=0)

    pieces = sems.shape[1]
    size = stage.shape[1] // pieces

    def send(s, p):
        rows = pl.ds(p * size, size)
        return pltpu.make_async_copy(stage.at[s, rows], out_hbm.at[s, rows], sems.at[s, p])

    scales = []
    for j in range(groups):
        norm0 = total[0:1, group_cols(j)]
        step = norm0 / total[1:2, group_cols(j)]
        norm1 = second[0:1, group_cols(j)]
        beta = norm1 / norm0
        step2 = norm1 / (second[1:2, group_cols(j)] - beta * norm1 / step)
        scales.append((step + step2 * (1.0 + beta), step2 * step))
    for s in range(subs):
        for p in range(pieces):
            rows = slice(p * size, (p + 1) * size)
            for j in range(groups):
                image, cols = (image_a, group_cols(j)) if j + 1 < groups else (image_b, group_cols(0))
                stage[s, rows, group_cols(j)] = scales[j][0] * loads[j][s, rows] - scales[j][1] * image[s, rows, cols]
            send(s, p).start()
    for s in range(subs):
        for p in range(pieces):
            send(s, p).wait()


def call(kernel, in_specs, outs, scratch=(), limit=5, in_hbm=(), alias=None):
    return pl.pallas_call(
        kernel,
        in_specs=in_specs,
        out_specs=[ANY if i in in_hbm else VMEM for i in range(len(outs))],
        out_shape=outs,
        scratch_shapes=list(scratch),
        input_output_aliases=alias or {},
        compiler_params=pltpu.CompilerParams(vmem_limit_bytes=limit * 2**20),
    )


def iterate(schur, mortar, partner, corner_map, coarse_inv, load):
    subs, order, columns = load.shape
    faces, block = mortar.shape[1], mortar.shape[2]
    half = faces // 2
    slots = subs * half
    coarse = coarse_inv.shape[1]
    groups = columns // LANES
    dma = pltpu.SemaphoreType.DMA
    table_scratch = [pltpu.SMEM(partner.shape, partner.dtype), pltpu.SMEM(corner_map.shape, corner_map.dtype)]
    tables = (hbm(partner), hbm(corner_map))

    def traces_of(width):
        return pltpu.VMEM((slots, block, width), BF16)

    loads, norms, ups, lows, csums, aboves, belows = [], [], [], [], [], [], []
    held_mortar = hbm(mortar)
    lead = call(
        lead_traces, [ANY, ANY], [traces_of(LANES)],
        [pltpu.VMEM((subs, half * block, LANES), F32), pltpu.VMEM((subs, half, block, block), BF16),
         dma((2, subs))],
    )(hbm(load), held_mortar)[0]
    aboves.append(vmem(shifted(lead, "sub", -1)))
    for j in range(groups):
        outs = [pltpu.VMEM((subs, order, LANES), F32)]
        if j == 0:
            outs.append(pltpu.VMEM(mortar.shape, BF16))
        outs += [traces_of(LANES)] * (1 + (j > 0)) + [pltpu.VMEM((8, LANES), F32), pltpu.VMEM((coarse, LANES), F32)]
        got = list(call(
            functools.partial(first_traces, j * LANES, j == 0),
            [ANY, ANY, ANY, ANY if j == 0 else VMEM], outs, table_scratch + [dma((3, max(subs, 2)))],
        )(*tables, hbm(load), held_mortar))
        loads.append(vmem(got.pop(0)))
        if j == 0:
            held_mortar = vmem(got.pop(0))
        if j == 0:
            got.insert(1, lead)
        belows.append(vmem(shifted(got[0], "sub", 1)))
        if j:
            aboves.append(vmem(shifted(got[1], "sub", -1)))
        ups.append(vmem(got[0]))
        lows.append(vmem(got[1]))
        norms.append(vmem(got[2]))
        csums.append(got[3])
    csum = vmem(group_sum(jnp.concatenate(csums, axis=1), "grp"))

    *stiff, held_schur, flipped = call(
        stiff_product, [ANY] + [VMEM] * (1 + groups),
        [pltpu.VMEM((subs, order, w), F32) for w in (columns - LANES, LANES)]
        + [pltpu.VMEM(schur.shape, BF16), pltpu.VMEM(mortar.shape, BF16)], [dma((subs,))],
    )(hbm(schur), held_mortar, *loads)
    held_schur, flipped = vmem(held_schur), vmem(flipped)

    bounds = ((0, groups - 1), (groups - 1, groups))
    share = 1.0 / lax.axis_size("grp")
    images, jumps, low2s, recvs, csum2s, tails = [], [], [], [], [], []
    tail, lead_slots = 2 * slots // 16, 4 * slots // 16
    cuts = ((slots - tail, tail), ((groups - 1) * tail + lead_slots, slots - lead_slots))
    for k, (lo, hi) in enumerate(bounds):
        n, w = hi - lo, (hi - lo) * LANES
        pick = [x[lo:hi] for x in (loads, norms, ups, lows, aboves, belows)]
        got = call(
            functools.partial(first_image, lo * LANES, n, groups, share),
            [ANY, ANY] + [VMEM] * (6 + 6 * n + k),
            [pltpu.VMEM((subs, order, w), F32)]
            + [pltpu.VMEM((size, block, w), BF16) for size in cuts[k]]
            + [traces_of(w)] * 2 + [pltpu.VMEM((coarse + 8, w), F32)],
            [pltpu.VMEM((coarse, w), F32), traces_of(w)] + table_scratch + [dma((2,))], alias={4: 0},
        )(*tables, held_mortar, flipped, vmem(stiff[k]), csum, coarse_inv, *sum(pick, []), csum2s[0] if k else csum, *tails)
        image, *up2, low2, jump, sums = got
        images.append(vmem(image))
        low2s.append(vmem(low2))
        jumps.append(vmem(jump))
        sums = group_sum(sums, "grp")
        if not k:
            csum, sums = lax.optimization_barrier((csum, sums))
            csum = vmem(csum)
        csum2s.append(vmem(sums))
        held = up2.pop() if not k else None
        tails = [vmem(held)] if not k else []
        for piece in up2:
            recvs.append(vmem(shifted(piece, "sub", 1)))

    totals = [vmem(x) for x in hub_sum(sums[coarse:], "sub")]
    hops = len(totals)
    total, norm1, energy = call(
        functools.partial(residual_sums, share, hops, groups),
        [VMEM] * (hops + 11 + groups), [pltpu.VMEM((8, columns), F32)] * 3, [pltpu.VMEM((order, columns), F32)],
    )(*totals, held_schur, csum, coarse_inv, *csum2s, *images, *loads, low2s[0], jumps[0], *recvs[:2])
    total, norm1, energy = vmem(total), vmem(norm1), vmem(energy)

    devices = lax.axis_size("sub") * lax.axis_size("grp")
    spread = call(
        last_sums, [VMEM] * 7, [pltpu.VMEM((devices, 2, columns), F32)],
    )(total, norm1, energy, low2s[1], jumps[1], *recvs[1:])[0]
    gathered = lax.all_to_all(spread, ("sub", "grp"), 0, 0, tiled=True)

    return call(
        finish, [VMEM] * (4 + groups),
        [jax.ShapeDtypeStruct((subs, order, columns), F32)],
        [pltpu.VMEM((subs, order, columns), F32), dma((subs, 2))], limit=9, in_hbm=(0,),
    )(total, vmem(gathered), *loads, *images)[0]


def solution(mesh):
    return jax.shard_map(
        iterate,
        mesh=mesh,
        in_specs=(
            P(("sub", "grp"), None, None),
            P(("sub", "grp"), None, None, None),
            P(("sub", "grp"), None),
            P(("sub", "grp"), None),
            P("sub", None, None),
            P(("sub", "grp"), None, None),
        ),
        out_specs=P(("sub", "grp"), None, None),
        check_vma=False,
    )
```

```python
import functools

import jax
import jax.numpy as jnp
from jax import lax
from jax.experimental import pallas as pl
from jax.experimental.pallas import tpu as pltpu
from jax.sharding import PartitionSpec as P


LANES = 128
F32 = jnp.float32
BF16 = jnp.bfloat16


def shifted(block, axis, distance):
    devices = range(lax.axis_size(axis))
    route = [((i - distance) % len(devices), i) for i in devices]
    return lax.ppermute(block, axis, route)


def group_sum(value, axis):
    size = lax.axis_size(axis)
    hop = 1
    while hop < size:
        value = value + lax.ppermute(value, axis, [(i ^ hop, i) for i in range(size)])
        hop *= 2
    return value


def hub_sum(value, axis):
    size = lax.axis_size(axis)
    hub = size - 1
    total = value
    for d in range(hub, 0, -1):
        route = [(i, (i + d) % size) for i in range(size) if (i + d) % size >= hub - 1]
        total = total + lax.ppermute(value, axis, route)
    others = [lax.ppermute(total, axis, [(hub, i)]) for i in reversed(range(hub - 1))]
    return [total] + others


def fold_rows(x):
    return jnp.sum(x.reshape(x.shape[0] // 8, 8, x.shape[1]), axis=0)


def vmem(x):
    return pltpu.with_memory_space_constraint(x, pltpu.VMEM)


def hbm(x):
    return pltpu.with_memory_space_constraint(x, pltpu.HBM)


VMEM = pl.BlockSpec(memory_space=pltpu.VMEM)
ANY = pl.BlockSpec(memory_space=pl.ANY)


def row_sum(x):
    return jnp.sum(x, axis=0, keepdims=True)


def group_cols(j):
    return slice(j * LANES, (j + 1) * LANES)


def fetch_tables(partner_hbm, cmap_hbm, partner, cmap, sems):
    return [
        pltpu.make_async_copy(partner_hbm, partner, sems.at[0]),
        pltpu.make_async_copy(cmap_hbm, cmap, sems.at[1]),
    ]


def lead_traces(load_hbm, mortar_hbm, low, load, mortar, sems):
    subs, half, block = mortar.shape[:3]
    width = load.shape[2]

    def fetch(s):
        rows = pl.ds(half * block, half * block)
        return [
            pltpu.make_async_copy(load_hbm.at[s, rows, pl.ds(0, width)], load.at[s], sems.at[0, s]),
            pltpu.make_async_copy(mortar_hbm.at[s, pl.ds(half, half)], mortar.at[s], sems.at[1, s]),
        ]

    for s in range(subs):
        for move in fetch(s):
            move.start()
    for s in range(subs):
        for move in fetch(s):
            move.wait()
        for f in range(half):
            rows = load[s, f * block : (f + 1) * block, :].astype(BF16)
            low[s * half + f] = jnp.dot(mortar[s, f], rows, preferred_element_type=F32).astype(BF16)


def first_traces(lo, copies, partner_hbm, cmap_hbm, load_hbm, mortar_in, *refs):
    if copies:
        load, mortar, up, norm, csum, partner, cmap, sems = refs
    else:
        load, up, low, norm, csum, partner, cmap, sems = refs
        mortar = mortar_in
    subs, order, width = load.shape
    faces, block = mortar.shape[1], mortar.shape[2]
    half = faces // 2
    corners = cmap.shape[1]
    stride = order // corners

    def fetch(s):
        moves = [pltpu.make_async_copy(load_hbm.at[s, :, pl.ds(lo, width)], load.at[s], sems.at[0, s])]
        if copies:
            moves.append(pltpu.make_async_copy(mortar_in.at[s], mortar.at[s], sems.at[1, s]))
        return moves

    tables = fetch_tables(partner_hbm, cmap_hbm, partner, cmap, sems.at[2])
    for move in tables:
        move.start()
    for s in range(subs):
        for move in fetch(s):
            move.start()
    norm[...] = jnp.zeros_like(norm)
    csum[...] = jnp.zeros_like(csum)
    for move in tables:
        move.wait()
    for s in range(subs):
        for move in fetch(s):
            move.wait()
        for f in range(faces):
            rows = load[s, f * block : (f + 1) * block, :]
            norm[...] += fold_rows(rows * rows)
            if copies and f >= half:
                continue
            trace = jnp.dot(mortar[s, f], rows.astype(BF16), preferred_element_type=F32).astype(BF16)
            if f < half:
                up[partner[s, f]] = trace
            else:
                low[s * half + f - half] = trace
        for c in range(corners):
            row = pl.ds(cmap[s, c], 1)
            csum[row, :] += load[s, c * stride : c * stride + 1, :]


def stiff_product(schur_hbm, mortar, *refs):
    loads, (out_a, out_b, schur, flipped, sems) = refs[:-5], refs[-5:]
    subs = schur.shape[0]

    def fetch(s):
        return pltpu.make_async_copy(schur_hbm.at[s], schur.at[s], sems.at[s])

    for s in range(subs):
        fetch(s).start()

    def work(s, _):
        fetch(s).wait()
        value = jnp.concatenate([load[s].astype(BF16) for load in loads], axis=1)
        product = jnp.dot(schur[s], value, preferred_element_type=F32)
        out_a[s] = product[:, : out_a.shape[2]]
        out_b[s] = product[:, out_a.shape[2] :]
        for f in range(mortar.shape[1]):
            flipped[s, f] = mortar[s, f].T
        return 0

    lax.fori_loop(0, subs, work, 0)


def first_image(lo, pieces, groups, share, partner_hbm, cmap_hbm, mortar, flipped, stiff, csum, cinv, *refs):
    ins, earlier, refs = refs[: 6 * pieces], refs[6 * pieces], refs[6 * pieces + 1 :]
    loads, norms, ups, lows, aboves, belows = (ins[i * pieces : (i + 1) * pieces] for i in range(6))
    tail_in, (send, rest), refs = refs[:-11], refs[-10:-8], refs[-11:-10] + refs[-8:]
    image, low_out, jump_out, sums, cval, up_out, partner, cmap, sems = refs
    subs, order, width = image.shape
    faces, block = mortar.shape[1], mortar.shape[2]
    half = faces // 2
    corners = cmap.shape[1]
    coarse = csum.shape[0]
    stride = order // corners
    cols = slice(lo, lo + width)
    tables = fetch_tables(partner_hbm, cmap_hbm, partner, cmap, sems)
    for move in tables:
        move.start()
    sums[...] = jnp.zeros_like(sums)
    cval[...] = jnp.dot(cinv[0], csum[:, cols], precision=lax.Precision.HIGHEST, preferred_element_type=F32)
    for move in tables:
        move.wait()

    def difference(own, other, slot):
        return jnp.concatenate(
            [(a[slot].astype(F32) - b[slot].astype(F32)).astype(BF16) for a, b in zip(own, other)], axis=1
        )

    def work(s, curv):
        for f in range(faces):
            if f < half:
                jump = difference(ups, aboves, partner[s, f])
            else:
                jump = difference(lows, belows, s * half + f - half)
                jump_out[s * half + f - half] = jump
            pulled = jnp.dot(flipped[s, f], jump, preferred_element_type=F32)
            rows = slice(f * block, (f + 1) * block)
            image[s, rows, :] = stiff[s, rows, :] + pulled
        for c in range(corners):
            row = pl.ds(cmap[s, c], 1)
            at = slice(c * stride, c * stride + 1)
            value = image[s, at, :] + cval[row, :]
            image[s, at, :] = value
            sums[row, :] += value
        for f in range(faces):
            at = slice(f * block, (f + 1) * block)
            rows = image[s, at, :]
            curv = tuple(
                acc + fold_rows(load[s, at, :] * rows[:, group_cols(j)])
                for j, (acc, load) in enumerate(zip(curv, loads))
            )
            trace = jnp.dot(mortar[s, f], rows.astype(BF16), preferred_element_type=F32).astype(BF16)
            if f < half:
                up_out[partner[s, f]] = trace
            else:
                low_out[s * half + f - half] = trace
        return curv

    curv = lax.fori_loop(0, subs, work, tuple(jnp.zeros((8, LANES), F32) for _ in loads))
    first = lo // LANES
    if first:
        kept = first * tail_in[0].shape[0]
        for at in range(kept):
            send[at] = tail_in[0][at // first, :, group_cols(at % first)]
        send[kept:] = up_out[: send.shape[0] - kept]
    else:
        send[...] = up_out[: send.shape[0]]
    rest[...] = up_out[up_out.shape[0] - rest.shape[0] :]
    for j in range(pieces):
        for row, value in ((first + j, norms[j][...]), (groups + first + j, curv[j])):
            sums[coarse + row : coarse + row + 1, :LANES] = row_sum(value)
    for j in range(first):
        for row in (j, groups + j):
            at = slice(coarse + row, coarse + row + 1)
            sums[at, :] = share * earlier[at, :LANES]


def residual_sums(share, hops, groups, *refs):
    parts, refs = refs[:hops], refs[hops:]
    schur, csum, cinv, csum_a, csum_b, image_a, image_b = refs[:7]
    loads, (low, jump), refs = refs[7 : 7 + groups], refs[7 + groups : 9 + groups], refs[9 + groups :]
    recvs, (total, norm, energy, resid) = refs[:-4], refs[-4:]
    coarse = csum.shape[0]
    value = jnp.where(lax.axis_index("sub") + 1 >= hops, parts[0][...], 0.0)
    for ref in parts[1:]:
        value += ref[...]
    for j in range(groups):
        total[0:1, group_cols(j)] = value[j : j + 1, :]
        total[1:2, group_cols(j)] = value[groups + j : groups + j + 1, :]
    step = total[0:1, :] / total[1:2, :]
    inner = jnp.concatenate([csum_a[:coarse, :], csum_b[:coarse, :]], axis=1)
    change = csum[...] - step * inner
    field = jnp.dot(cinv[0], change, precision=lax.Precision.HIGHEST, preferred_element_type=F32)
    norm[...] = jnp.zeros_like(norm)
    energy[...] = share * fold_rows(change * field)

    slots, subs, order = low.shape[0], schur.shape[0], schur.shape[1]
    tile = min(256, order)

    def received(k, j):
        whole, mixed = recvs
        if k < whole.shape[0]:
            return whole[k, :, group_cols(j)]
        return mixed[(k - whole.shape[0]) * (groups - 1) + j]

    for s in range(subs):
        for j, load in enumerate(loads):
            cols = group_cols(j)
            image, own = (image_a, cols) if j + 1 < groups else (image_b, group_cols(0))
            resid[:, cols] = load[s] - step[:, cols] * image[s, :, own]
        r = resid[...]
        norm[...] += fold_rows(r * r)
        half = r.astype(BF16)
        for i in range(0, order, tile):
            rows = slice(i, i + tile)
            beyond = half[rows, :]
            if i + tile < order:
                beyond = jnp.concatenate([beyond, half[i + tile :, :] * BF16(2.0)], axis=0)
            product = jnp.dot(schur[s, rows, i:], beyond, preferred_element_type=F32)
            energy[...] += fold_rows(r[rows, :] * product)
        for j in range(groups - 1):
            cols = group_cols(j)
            acc = energy[:, cols]
            for k in range(s * slots // subs, (s + 1) * slots // subs):
                delta = low[k, :, cols].astype(F32) - received(k, j).astype(F32)
                value = jump[k, :, cols].astype(F32) - step[:, cols] * delta
                acc += fold_rows(value * value)
            energy[:, cols] = acc


def jump_squares(step, low, jump, recvs, cols):
    acc, start = jnp.zeros((8, LANES), F32), low.shape[0] - sum(recv.shape[0] for recv in recvs)
    for recv in recvs:

        def one(k, acc, recv=recv, start=start):
            delta = low[start + k, :, cols].astype(F32) - recv[k, :, cols].astype(F32)
            value = jump[start + k, :, cols].astype(F32) - step * delta
            return acc + fold_rows(value * value)

        acc = lax.fori_loop(max(-start, 0), recv.shape[0], one, acc, unroll=2)
        start += recv.shape[0]
    return acc


def last_sums(total, norm, energy, low, jump, *refs):
    recvs, out = refs[:-1], refs[-1]
    groups = norm.shape[1] // LANES
    last = group_cols(groups - 1)
    step = total[0:1, last] / total[1:2, last]
    ending = row_sum(energy[:, last] + jump_squares(step, low, jump, recvs, group_cols(0)))
    for d in range(out.shape[0]):
        out[d, 0:1, :] = row_sum(norm[...])
        out[d, 1:2, :] = row_sum(energy[...])
        out[d, 1:2, last] = ending


def finish(total, gathered, *refs):
    loads, (image_a, image_b, out_hbm, stage, sems) = refs[:-5], refs[-5:]
    groups = len(loads)
    subs = stage.shape[0]
    second = jnp.sum(gathered[...], axis=0)

    pieces = sems.shape[1]
    size = stage.shape[1] // pieces

    def send(s, p):
        rows = pl.ds(p * size, size)
        return pltpu.make_async_copy(stage.at[s, rows], out_hbm.at[s, rows], sems.at[s, p])

    scales = []
    for j in range(groups):
        norm0 = total[0:1, group_cols(j)]
        step = norm0 / total[1:2, group_cols(j)]
        norm1 = second[0:1, group_cols(j)]
        beta = norm1 / norm0
        step2 = norm1 / (second[1:2, group_cols(j)] - beta * norm1 / step)
        scales.append((step + step2 * (1.0 + beta), step2 * step))
    for s in range(subs):
        for p in range(pieces):
            rows = slice(p * size, (p + 1) * size)
            for j in range(groups):
                image, cols = (image_a, group_cols(j)) if j + 1 < groups else (image_b, group_cols(0))
                stage[s, rows, group_cols(j)] = scales[j][0] * loads[j][s, rows] - scales[j][1] * image[s, rows, cols]
            send(s, p).start()
    for s in range(subs):
        for p in range(pieces):
            send(s, p).wait()


def call(kernel, in_specs, outs, scratch=(), limit=5, in_hbm=(), alias=None):
    return pl.pallas_call(
        kernel,
        in_specs=in_specs,
        out_specs=[ANY if i in in_hbm else VMEM for i in range(len(outs))],
        out_shape=outs,
        scratch_shapes=list(scratch),
        input_output_aliases=alias or {},
        compiler_params=pltpu.CompilerParams(vmem_limit_bytes=limit * 2**20),
    )


def iterate(schur, mortar, partner, corner_map, coarse_inv, load):
    subs, order, columns = load.shape
    faces, block = mortar.shape[1], mortar.shape[2]
    half = faces // 2
    slots = subs * half
    coarse = coarse_inv.shape[1]
    groups = columns // LANES
    dma = pltpu.SemaphoreType.DMA
    table_scratch = [pltpu.SMEM(partner.shape, partner.dtype), pltpu.SMEM(corner_map.shape, corner_map.dtype)]
    tables = (hbm(partner), hbm(corner_map))

    def traces_of(width):
        return pltpu.VMEM((slots, block, width), BF16)

    loads, norms, ups, lows, csums, aboves, belows = [], [], [], [], [], [], []
    held_mortar = hbm(mortar)
    lead = call(
        lead_traces, [ANY, ANY], [traces_of(LANES)],
        [pltpu.VMEM((subs, half * block, LANES), F32), pltpu.VMEM((subs, half, block, block), BF16),
         dma((2, subs))],
    )(hbm(load), held_mortar)[0]
    aboves.append(vmem(shifted(lead, "sub", -1)))
    for j in range(groups):
        outs = [pltpu.VMEM((subs, order, LANES), F32)]
        if j == 0:
            outs.append(pltpu.VMEM(mortar.shape, BF16))
        outs += [traces_of(LANES)] * (1 + (j > 0)) + [pltpu.VMEM((8, LANES), F32), pltpu.VMEM((coarse, LANES), F32)]
        got = list(call(
            functools.partial(first_traces, j * LANES, j == 0),
            [ANY, ANY, ANY, ANY if j == 0 else VMEM], outs, table_scratch + [dma((3, max(subs, 2)))],
        )(*tables, hbm(load), held_mortar))
        loads.append(vmem(got.pop(0)))
        if j == 0:
            held_mortar = vmem(got.pop(0))
        if j == 0:
            got.insert(1, lead)
        belows.append(vmem(shifted(got[0], "sub", 1)))
        if j:
            aboves.append(vmem(shifted(got[1], "sub", -1)))
        ups.append(vmem(got[0]))
        lows.append(vmem(got[1]))
        norms.append(vmem(got[2]))
        csums.append(got[3])
    csum = vmem(group_sum(jnp.concatenate(csums, axis=1), "grp"))

    *stiff, held_schur, flipped = call(
        stiff_product, [ANY] + [VMEM] * (1 + groups),
        [pltpu.VMEM((subs, order, w), F32) for w in (columns - LANES, LANES)]
        + [pltpu.VMEM(schur.shape, BF16), pltpu.VMEM(mortar.shape, BF16)], [dma((subs,))],
    )(hbm(schur), held_mortar, *loads)
    held_schur, flipped = vmem(held_schur), vmem(flipped)

    bounds = ((0, groups - 1), (groups - 1, groups))
    share = 1.0 / lax.axis_size("grp")
    images, jumps, low2s, recvs, csum2s, tails = [], [], [], [], [], []
    tail, lead_slots = slots // 16, 6 * slots // 16
    cuts = ((slots - tail, tail), ((groups - 1) * tail + lead_slots, slots - lead_slots))
    for k, (lo, hi) in enumerate(bounds):
        n, w = hi - lo, (hi - lo) * LANES
        pick = [x[lo:hi] for x in (loads, norms, ups, lows, aboves, belows)]
        got = call(
            functools.partial(first_image, lo * LANES, n, groups, share),
            [ANY, ANY] + [VMEM] * (6 + 6 * n + k),
            [pltpu.VMEM((subs, order, w), F32)]
            + [pltpu.VMEM((size, block, w), BF16) for size in cuts[k]]
            + [traces_of(w)] * 2 + [pltpu.VMEM((coarse + 8, w), F32)],
            [pltpu.VMEM((coarse, w), F32), traces_of(w)] + table_scratch + [dma((2,))], alias={4: 0},
        )(*tables, held_mortar, flipped, vmem(stiff[k]), csum, coarse_inv, *sum(pick, []), csum2s[0] if k else csum, *tails)
        image, *up2, low2, jump, sums = got
        images.append(vmem(image))
        low2s.append(vmem(low2))
        jumps.append(vmem(jump))
        sums = group_sum(sums, "grp")
        if not k:
            csum, sums = lax.optimization_barrier((csum, sums))
            csum = vmem(csum)
        csum2s.append(vmem(sums))
        held = up2.pop() if not k else None
        tails = [vmem(held)] if not k else []
        for piece in up2:
            recvs.append(vmem(shifted(piece, "sub", 1)))

    totals = [vmem(x) for x in hub_sum(sums[coarse:], "sub")]
    hops = len(totals)
    total, norm1, energy = call(
        functools.partial(residual_sums, share, hops, groups),
        [VMEM] * (hops + 11 + groups), [pltpu.VMEM((8, columns), F32)] * 3, [pltpu.VMEM((order, columns), F32)],
    )(*totals, held_schur, csum, coarse_inv, *csum2s, *images, *loads, low2s[0], jumps[0], *recvs[:2])
    total, norm1, energy = vmem(total), vmem(norm1), vmem(energy)

    devices = lax.axis_size("sub") * lax.axis_size("grp")
    spread = call(
        last_sums, [VMEM] * 7, [pltpu.VMEM((devices, 2, columns), F32)],
    )(total, norm1, energy, low2s[1], jumps[1], *recvs[1:])[0]
    gathered = lax.all_to_all(spread, ("sub", "grp"), 0, 0, tiled=True)

    return call(
        finish, [VMEM] * (4 + groups),
        [jax.ShapeDtypeStruct((subs, order, columns), F32)],
        [pltpu.VMEM((subs, order, columns), F32), dma((subs, 2))], limit=9, in_hbm=(0,),
    )(total, vmem(gathered), *loads, *images)[0]


def solution(mesh):
    return jax.shard_map(
        iterate,
        mesh=mesh,
        in_specs=(
            P(("sub", "grp"), None, None),
            P(("sub", "grp"), None, None, None),
            P(("sub", "grp"), None),
            P(("sub", "grp"), None),
            P("sub", None, None),
            P(("sub", "grp"), None, None),
        ),
        out_specs=P(("sub", "grp"), None, None),
        check_vma=False,
    )
```

```python
import functools

import jax
import jax.numpy as jnp
from jax import lax
from jax.experimental import pallas as pl
from jax.experimental.pallas import tpu as pltpu
from jax.sharding import PartitionSpec as P


LANES = 128
F32 = jnp.float32
BF16 = jnp.bfloat16


def shifted(block, axis, distance):
    devices = range(lax.axis_size(axis))
    route = [((i - distance) % len(devices), i) for i in devices]
    return lax.ppermute(block, axis, route)


def group_sum(value, axis):
    size = lax.axis_size(axis)
    hop = 1
    while hop < size:
        value = value + lax.ppermute(value, axis, [(i ^ hop, i) for i in range(size)])
        hop *= 2
    return value


def hub_sum(value, axis):
    size = lax.axis_size(axis)
    hub = size - 1
    total = value
    for d in range(hub, 0, -1):
        route = [(i, (i + d) % size) for i in range(size) if (i + d) % size >= hub - 1]
        total = total + lax.ppermute(value, axis, route)
    others = [lax.ppermute(total, axis, [(hub, i)]) for i in reversed(range(hub - 1))]
    return [total] + others


def fold_rows(x):
    return jnp.sum(x.reshape(x.shape[0] // 8, 8, x.shape[1]), axis=0)


def vmem(x):
    return pltpu.with_memory_space_constraint(x, pltpu.VMEM)


def hbm(x):
    return pltpu.with_memory_space_constraint(x, pltpu.HBM)


VMEM = pl.BlockSpec(memory_space=pltpu.VMEM)
ANY = pl.BlockSpec(memory_space=pl.ANY)


def row_sum(x):
    return jnp.sum(x, axis=0, keepdims=True)


def group_cols(j):
    return slice(j * LANES, (j + 1) * LANES)


def fetch_tables(partner_hbm, cmap_hbm, partner, cmap, sems):
    return [
        pltpu.make_async_copy(partner_hbm, partner, sems.at[0]),
        pltpu.make_async_copy(cmap_hbm, cmap, sems.at[1]),
    ]


def lead_traces(load_hbm, mortar_hbm, low, load, mortar, sems):
    subs, half, block = mortar.shape[:3]
    width = load.shape[2]

    def fetch(s):
        rows = pl.ds(half * block, half * block)
        return [
            pltpu.make_async_copy(load_hbm.at[s, rows, pl.ds(0, width)], load.at[s], sems.at[0, s]),
            pltpu.make_async_copy(mortar_hbm.at[s, pl.ds(half, half)], mortar.at[s], sems.at[1, s]),
        ]

    for s in range(subs):
        for move in fetch(s):
            move.start()
    for s in range(subs):
        for move in fetch(s):
            move.wait()
        for f in range(half):
            rows = load[s, f * block : (f + 1) * block, :].astype(BF16)
            low[s * half + f] = jnp.dot(mortar[s, f], rows, preferred_element_type=F32).astype(BF16)


def first_traces(lo, copies, partner_hbm, cmap_hbm, load_hbm, mortar_in, *refs):
    if copies:
        load, mortar, up, low, norm, csum, partner, cmap, sems = refs
    else:
        load, up, low, norm, csum, partner, cmap, sems = refs
        mortar = mortar_in
    subs, order, width = load.shape
    faces, block = mortar.shape[1], mortar.shape[2]
    half = faces // 2
    corners = cmap.shape[1]
    stride = order // corners

    def fetch(s):
        moves = [pltpu.make_async_copy(load_hbm.at[s, :, pl.ds(lo, width)], load.at[s], sems.at[0, s])]
        if copies:
            moves.append(pltpu.make_async_copy(mortar_in.at[s], mortar.at[s], sems.at[1, s]))
        return moves

    tables = fetch_tables(partner_hbm, cmap_hbm, partner, cmap, sems.at[2])
    for move in tables:
        move.start()
    for s in range(subs):
        for move in fetch(s):
            move.start()
    norm[...] = jnp.zeros_like(norm)
    csum[...] = jnp.zeros_like(csum)
    for move in tables:
        move.wait()
    for s in range(subs):
        for move in fetch(s):
            move.wait()
        for f in range(faces):
            rows = load[s, f * block : (f + 1) * block, :]
            norm[...] += fold_rows(rows * rows)
            if copies and (f >= half and s < subs // 2):
                continue
            trace = jnp.dot(mortar[s, f], rows.astype(BF16), preferred_element_type=F32).astype(BF16)
            if f < half:
                up[partner[s, f]] = trace
            else:
                low[(s - subs // 2 if copies else s) * half + f - half] = trace
        for c in range(corners):
            row = pl.ds(cmap[s, c], 1)
            csum[row, :] += load[s, c * stride : c * stride + 1, :]


def stiff_product(schur_hbm, mortar, *refs):
    loads, (out_a, out_b, schur, flipped, sems) = refs[:-5], refs[-5:]
    subs = schur.shape[0]

    def fetch(s):
        return pltpu.make_async_copy(schur_hbm.at[s], schur.at[s], sems.at[s])

    for s in range(subs):
        fetch(s).start()

    def work(s, _):
        fetch(s).wait()
        value = jnp.concatenate([load[s].astype(BF16) for load in loads], axis=1)
        product = jnp.dot(schur[s], value, preferred_element_type=F32)
        out_a[s] = product[:, : out_a.shape[2]]
        out_b[s] = product[:, out_a.shape[2] :]
        for f in range(mortar.shape[1]):
            flipped[s, f] = mortar[s, f].T
        return 0

    lax.fori_loop(0, subs, work, 0)


def first_image(lo, pieces, groups, share, partner_hbm, cmap_hbm, mortar, flipped, stiff, csum, cinv, *refs):
    ins, earlier, refs = refs[: 6 * pieces], refs[6 * pieces], refs[6 * pieces + 1 :]
    loads, norms, ups, lows, aboves, belows = (ins[i * pieces : (i + 1) * pieces] for i in range(6))
    refs, joined = refs[:-2], refs[-2:]
    tail_in, (send, rest), refs = refs[:-11], refs[-10:-8], refs[-11:-10] + refs[-8:]
    image, low_out, jump_out, sums, cval, up_out, partner, cmap, sems = refs
    subs, order, width = image.shape
    faces, block = mortar.shape[1], mortar.shape[2]
    half = faces // 2
    corners = cmap.shape[1]
    coarse = csum.shape[0]
    stride = order // corners
    cols = slice(lo, lo + width)
    if not lo:
        for whole, start, more in zip(joined, (lows[0], aboves[0]), tail_in):
            whole[: start.shape[0]] = start[...]
            whole[start.shape[0] :] = more[...]
        lows, aboves = joined[:1] + lows[1:], joined[1:] + aboves[1:]
    tables = fetch_tables(partner_hbm, cmap_hbm, partner, cmap, sems)
    for move in tables:
        move.start()
    sums[...] = jnp.zeros_like(sums)
    cval[...] = jnp.dot(cinv[0], csum[:, cols], precision=lax.Precision.HIGHEST, preferred_element_type=F32)
    for move in tables:
        move.wait()

    def difference(own, other, slot):
        return jnp.concatenate(
            [(a[slot].astype(F32) - b[slot].astype(F32)).astype(BF16) for a, b in zip(own, other)], axis=1
        )

    def work(s, curv):
        for f in range(faces):
            if f < half:
                jump = difference(ups, aboves, partner[s, f])
            else:
                jump = difference(lows, belows, s * half + f - half)
                jump_out[s * half + f - half] = jump
            pulled = jnp.dot(flipped[s, f], jump, preferred_element_type=F32)
            rows = slice(f * block, (f + 1) * block)
            image[s, rows, :] = stiff[s, rows, :] + pulled
        for c in range(corners):
            row = pl.ds(cmap[s, c], 1)
            at = slice(c * stride, c * stride + 1)
            value = image[s, at, :] + cval[row, :]
            image[s, at, :] = value
            sums[row, :] += value
        for f in range(faces):
            at = slice(f * block, (f + 1) * block)
            rows = image[s, at, :]
            curv = tuple(
                acc + fold_rows(load[s, at, :] * rows[:, group_cols(j)])
                for j, (acc, load) in enumerate(zip(curv, loads))
            )
            trace = jnp.dot(mortar[s, f], rows.astype(BF16), preferred_element_type=F32).astype(BF16)
            if f < half:
                up_out[partner[s, f]] = trace
            else:
                low_out[s * half + f - half] = trace
        return curv

    curv = lax.fori_loop(0, subs, work, tuple(jnp.zeros((8, LANES), F32) for _ in loads))
    first = lo // LANES
    if first:
        kept = first * tail_in[0].shape[0]
        for at in range(kept):
            send[at] = tail_in[0][at // first, :, group_cols(at % first)]
        send[kept:] = up_out[: send.shape[0] - kept]
    else:
        send[...] = up_out[: send.shape[0]]
    rest[...] = up_out[up_out.shape[0] - rest.shape[0] :]
    for j in range(pieces):
        for row, value in ((first + j, norms[j][...]), (groups + first + j, curv[j])):
            sums[coarse + row : coarse + row + 1, :LANES] = row_sum(value)
    for j in range(first):
        for row in (j, groups + j):
            at = slice(coarse + row, coarse + row + 1)
            sums[at, :] = share * earlier[at, :LANES]


def residual_sums(share, hops, groups, *refs):
    parts, refs = refs[:hops], refs[hops:]
    schur, csum, cinv, csum_a, csum_b, image_a, image_b = refs[:7]
    loads, (low, jump), refs = refs[7 : 7 + groups], refs[7 + groups : 9 + groups], refs[9 + groups :]
    recvs, (total, norm, energy, resid) = refs[:-4], refs[-4:]
    coarse = csum.shape[0]
    value = jnp.where(lax.axis_index("sub") + 1 >= hops, parts[0][...], 0.0)
    for ref in parts[1:]:
        value += ref[...]
    for j in range(groups):
        total[0:1, group_cols(j)] = value[j : j + 1, :]
        total[1:2, group_cols(j)] = value[groups + j : groups + j + 1, :]
    step = total[0:1, :] / total[1:2, :]
    inner = jnp.concatenate([csum_a[:coarse, :], csum_b[:coarse, :]], axis=1)
    change = csum[...] - step * inner
    field = jnp.dot(cinv[0], change, precision=lax.Precision.HIGHEST, preferred_element_type=F32)
    norm[...] = jnp.zeros_like(norm)
    energy[...] = share * fold_rows(change * field)

    slots, subs, order = low.shape[0], schur.shape[0], schur.shape[1]
    tile = min(256, order)

    def received(k, j):
        whole, mixed = recvs
        if k < whole.shape[0]:
            return whole[k, :, group_cols(j)]
        return mixed[(k - whole.shape[0]) * (groups - 1) + j]

    for s in range(subs):
        for j, load in enumerate(loads):
            cols = group_cols(j)
            image, own = (image_a, cols) if j + 1 < groups else (image_b, group_cols(0))
            resid[:, cols] = load[s] - step[:, cols] * image[s, :, own]
        r = resid[...]
        norm[...] += fold_rows(r * r)
        half = r.astype(BF16)
        for i in range(0, order, tile):
            rows = slice(i, i + tile)
            beyond = half[rows, :]
            if i + tile < order:
                beyond = jnp.concatenate([beyond, half[i + tile :, :] * BF16(2.0)], axis=0)
            product = jnp.dot(schur[s, rows, i:], beyond, preferred_element_type=F32)
            energy[...] += fold_rows(r[rows, :] * product)
        for j in range(groups - 1):
            cols = group_cols(j)
            acc = energy[:, cols]
            for k in range(s * slots // subs, (s + 1) * slots // subs):
                delta = low[k, :, cols].astype(F32) - received(k, j).astype(F32)
                value = jump[k, :, cols].astype(F32) - step[:, cols] * delta
                acc += fold_rows(value * value)
            energy[:, cols] = acc


def jump_squares(step, low, jump, recvs, cols):
    acc, start = jnp.zeros((8, LANES), F32), low.shape[0] - sum(recv.shape[0] for recv in recvs)
    for recv in recvs:

        def one(k, acc, recv=recv, start=start):
            delta = low[start + k, :, cols].astype(F32) - recv[k, :, cols].astype(F32)
            value = jump[start + k, :, cols].astype(F32) - step * delta
            return acc + fold_rows(value * value)

        acc = lax.fori_loop(max(-start, 0), recv.shape[0], one, acc, unroll=2)
        start += recv.shape[0]
    return acc


def last_sums(total, norm, energy, low, jump, *refs):
    recvs, out = refs[:-1], refs[-1]
    groups = norm.shape[1] // LANES
    last = group_cols(groups - 1)
    step = total[0:1, last] / total[1:2, last]
    ending = row_sum(energy[:, last] + jump_squares(step, low, jump, recvs, group_cols(0)))
    for d in range(out.shape[0]):
        out[d, 0:1, :] = row_sum(norm[...])
        out[d, 1:2, :] = row_sum(energy[...])
        out[d, 1:2, last] = ending


def finish(total, gathered, *refs):
    loads, (image_a, image_b, out_hbm, stage, sems) = refs[:-5], refs[-5:]
    groups = len(loads)
    subs = stage.shape[0]
    second = jnp.sum(gathered[...], axis=0)

    pieces = sems.shape[1]
    size = stage.shape[1] // pieces

    def send(s, p):
        rows = pl.ds(p * size, size)
        return pltpu.make_async_copy(stage.at[s, rows], out_hbm.at[s, rows], sems.at[s, p])

    scales = []
    for j in range(groups):
        norm0 = total[0:1, group_cols(j)]
        step = norm0 / total[1:2, group_cols(j)]
        norm1 = second[0:1, group_cols(j)]
        beta = norm1 / norm0
        step2 = norm1 / (second[1:2, group_cols(j)] - beta * norm1 / step)
        scales.append((step + step2 * (1.0 + beta), step2 * step))
    for s in range(subs):
        for p in range(pieces):
            rows = slice(p * size, (p + 1) * size)
            for j in range(groups):
                image, cols = (image_a, group_cols(j)) if j + 1 < groups else (image_b, group_cols(0))
                stage[s, rows, group_cols(j)] = scales[j][0] * loads[j][s, rows] - scales[j][1] * image[s, rows, cols]
            send(s, p).start()
    for s in range(subs):
        for p in range(pieces):
            send(s, p).wait()


def call(kernel, in_specs, outs, scratch=(), limit=5, in_hbm=(), alias=None):
    return pl.pallas_call(
        kernel,
        in_specs=in_specs,
        out_specs=[ANY if i in in_hbm else VMEM for i in range(len(outs))],
        out_shape=outs,
        scratch_shapes=list(scratch),
        input_output_aliases=alias or {},
        compiler_params=pltpu.CompilerParams(vmem_limit_bytes=limit * 2**20),
    )


def iterate(schur, mortar, partner, corner_map, coarse_inv, load):
    subs, order, columns = load.shape
    faces, block = mortar.shape[1], mortar.shape[2]
    half = faces // 2
    slots = subs * half
    coarse = coarse_inv.shape[1]
    groups = columns // LANES
    dma = pltpu.SemaphoreType.DMA
    table_scratch = [pltpu.SMEM(partner.shape, partner.dtype), pltpu.SMEM(corner_map.shape, corner_map.dtype)]
    tables = (hbm(partner), hbm(corner_map))

    def traces_of(width):
        return pltpu.VMEM((slots, block, width), BF16)

    loads, norms, ups, lows, csums, aboves, belows = [], [], [], [], [], [], []
    half_traces = pltpu.VMEM((slots // 2, block, LANES), BF16)
    held_mortar = hbm(mortar)
    lead = call(
        lead_traces, [ANY, ANY], [half_traces],
        [pltpu.VMEM((subs // 2, half * block, LANES), F32),
         pltpu.VMEM((subs // 2, half, block, block), BF16), dma((2, subs))],
    )(hbm(load), held_mortar)[0]
    aboves.append(vmem(shifted(lead, "sub", -1)))
    for j in range(groups):
        outs = [pltpu.VMEM((subs, order, LANES), F32)]
        if j == 0:
            outs.append(pltpu.VMEM(mortar.shape, BF16))
        outs += [traces_of(LANES), traces_of(LANES) if j else half_traces] + [pltpu.VMEM((8, LANES), F32), pltpu.VMEM((coarse, LANES), F32)]
        got = list(call(
            functools.partial(first_traces, j * LANES, j == 0),
            [ANY, ANY, ANY, ANY if j == 0 else VMEM], outs, table_scratch + [dma((3, max(subs, 2)))],
        )(*tables, hbm(load), held_mortar))
        loads.append(vmem(got.pop(0)))
        if j == 0:
            held_mortar = vmem(got.pop(0))
        above = vmem(shifted(got[1], "sub", -1))
        belows.append(vmem(shifted(got[0], "sub", 1)))
        if j:
            aboves.append(above)
        else:
            others, got[1] = [vmem(got[1]), above], lead
        ups.append(vmem(got[0]))
        lows.append(vmem(got[1]))
        norms.append(vmem(got[2]))
        csums.append(got[3])
    csum = vmem(group_sum(jnp.concatenate(csums, axis=1), "grp"))

    *stiff, held_schur, flipped = call(
        stiff_product, [ANY] + [VMEM] * (1 + groups),
        [pltpu.VMEM((subs, order, w), F32) for w in (columns - LANES, LANES)]
        + [pltpu.VMEM(schur.shape, BF16), pltpu.VMEM(mortar.shape, BF16)], [dma((subs,))],
    )(hbm(schur), held_mortar, *loads)
    held_schur, flipped = vmem(held_schur), vmem(flipped)

    bounds = ((0, groups - 1), (groups - 1, groups))
    share = 1.0 / lax.axis_size("grp")
    images, jumps, low2s, recvs, csum2s, tails = [], [], [], [], [], []
    tail, lead_slots = slots // 16, 6 * slots // 16
    cuts = ((slots - tail, tail), ((groups - 1) * tail + lead_slots, slots - lead_slots))
    for k, (lo, hi) in enumerate(bounds):
        n, w = hi - lo, (hi - lo) * LANES
        pick = [x[lo:hi] for x in (loads, norms, ups, lows, aboves, belows)]
        got = call(
            functools.partial(first_image, lo * LANES, n, groups, share),
            [ANY, ANY] + [VMEM] * (8 + 6 * n - k),
            [pltpu.VMEM((subs, order, w), F32)]
            + [pltpu.VMEM((size, block, w), BF16) for size in cuts[k]]
            + [traces_of(w)] * 2 + [pltpu.VMEM((coarse + 8, w), F32)],
            [pltpu.VMEM((coarse, w), F32), traces_of(w)] + table_scratch + [dma((2,))]
            + [traces_of(LANES)] * 2, alias={4: 0},
        )(*tables, held_mortar, flipped, vmem(stiff[k]), csum, coarse_inv, *sum(pick, []), csum2s[0] if k else csum, *(tails if k else others))
        image, *up2, low2, jump, sums = got
        images.append(vmem(image))
        low2s.append(vmem(low2))
        jumps.append(vmem(jump))
        sums = group_sum(sums, "grp")
        if not k:
            csum, sums = lax.optimization_barrier((csum, sums))
            csum = vmem(csum)
        csum2s.append(vmem(sums))
        held = up2.pop() if not k else None
        tails = [vmem(held)] if not k else []
        for piece in up2:
            recvs.append(vmem(shifted(piece, "sub", 1)))

    totals = [vmem(x) for x in hub_sum(sums[coarse:], "sub")]
    hops = len(totals)
    total, norm1, energy = call(
        functools.partial(residual_sums, share, hops, groups),
        [VMEM] * (hops + 11 + groups), [pltpu.VMEM((8, columns), F32)] * 3, [pltpu.VMEM((order, columns), F32)],
    )(*totals, held_schur, csum, coarse_inv, *csum2s, *images, *loads, low2s[0], jumps[0], *recvs[:2])
    total, norm1, energy = vmem(total), vmem(norm1), vmem(energy)

    devices = lax.axis_size("sub") * lax.axis_size("grp")
    spread = call(
        last_sums, [VMEM] * 7, [pltpu.VMEM((devices, 2, columns), F32)],
    )(total, norm1, energy, low2s[1], jumps[1], *recvs[1:])[0]
    gathered = lax.all_to_all(spread, ("sub", "grp"), 0, 0, tiled=True)

    return call(
        finish, [VMEM] * (4 + groups),
        [jax.ShapeDtypeStruct((subs, order, columns), F32)],
        [pltpu.VMEM((subs, order, columns), F32), dma((subs, 2))], limit=9, in_hbm=(0,),
    )(total, vmem(gathered), *loads, *images)[0]


def solution(mesh):
    return jax.shard_map(
        iterate,
        mesh=mesh,
        in_specs=(
            P(("sub", "grp"), None, None),
            P(("sub", "grp"), None, None, None),
            P(("sub", "grp"), None),
            P(("sub", "grp"), None),
            P("sub", None, None),
            P(("sub", "grp"), None, None),
        ),
        out_specs=P(("sub", "grp"), None, None),
        check_vma=False,
    )
```

```python
import functools

import jax
import jax.numpy as jnp
from jax import lax
from jax.experimental import pallas as pl
from jax.experimental.pallas import tpu as pltpu
from jax.sharding import PartitionSpec as P


LANES = 128
F32 = jnp.float32
BF16 = jnp.bfloat16


def shifted(block, axis, distance):
    devices = range(lax.axis_size(axis))
    route = [((i - distance) % len(devices), i) for i in devices]
    return lax.ppermute(block, axis, route)


def group_sum(value, axis):
    size = lax.axis_size(axis)
    hop = 1
    while hop < size:
        value = value + lax.ppermute(value, axis, [(i ^ hop, i) for i in range(size)])
        hop *= 2
    return value


def hub_sum(value, axis):
    size = lax.axis_size(axis)
    hub = size - 1
    total = value
    for d in range(hub, 0, -1):
        route = [(i, (i + d) % size) for i in range(size) if (i + d) % size >= hub - 1]
        total = total + lax.ppermute(value, axis, route)
    others = [lax.ppermute(total, axis, [(hub, i)]) for i in reversed(range(hub - 1))]
    return [total] + others


def fold_rows(x):
    return jnp.sum(x.reshape(x.shape[0] // 8, 8, x.shape[1]), axis=0)


def vmem(x):
    return pltpu.with_memory_space_constraint(x, pltpu.VMEM)


def hbm(x):
    return pltpu.with_memory_space_constraint(x, pltpu.HBM)


VMEM = pl.BlockSpec(memory_space=pltpu.VMEM)
ANY = pl.BlockSpec(memory_space=pl.ANY)


def row_sum(x):
    return jnp.sum(x, axis=0, keepdims=True)


def group_cols(j):
    return slice(j * LANES, (j + 1) * LANES)


def fetch_tables(partner_hbm, cmap_hbm, partner, cmap, sems):
    return [
        pltpu.make_async_copy(partner_hbm, partner, sems.at[0]),
        pltpu.make_async_copy(cmap_hbm, cmap, sems.at[1]),
    ]


def lead_traces(load_hbm, mortar_hbm, low, load, mortar, sems):
    subs, half, block = mortar.shape[:3]
    width = load.shape[2]

    def fetch(s):
        rows = pl.ds(half * block, half * block)
        return [
            pltpu.make_async_copy(load_hbm.at[s, rows, pl.ds(0, width)], load.at[s], sems.at[0, s]),
            pltpu.make_async_copy(mortar_hbm.at[s, pl.ds(half, half)], mortar.at[s], sems.at[1, s]),
        ]

    for s in range(subs):
        for move in fetch(s):
            move.start()
    for s in range(subs):
        for move in fetch(s):
            move.wait()
        for f in range(half):
            rows = load[s, f * block : (f + 1) * block, :].astype(BF16)
            low[s * half + f] = jnp.dot(mortar[s, f], rows, preferred_element_type=F32).astype(BF16)


def first_traces(lo, copies, partner_hbm, cmap_hbm, load_hbm, mortar_in, *refs):
    if copies:
        load, mortar, up, low, norm, csum, partner, cmap, sems = refs
    else:
        load, up, low, norm, csum, partner, cmap, sems = refs
        mortar = mortar_in
    subs, order, width = load.shape
    faces, block = mortar.shape[1], mortar.shape[2]
    half = faces // 2
    corners = cmap.shape[1]
    stride = order // corners

    def fetch(s):
        moves = [pltpu.make_async_copy(load_hbm.at[s, :, pl.ds(lo, width)], load.at[s], sems.at[0, s])]
        if copies:
            moves.append(pltpu.make_async_copy(mortar_in.at[s], mortar.at[s], sems.at[1, s]))
        return moves

    tables = fetch_tables(partner_hbm, cmap_hbm, partner, cmap, sems.at[2])
    for move in tables:
        move.start()
    for s in range(subs):
        for move in fetch(s):
            move.start()
    norm[...] = jnp.zeros_like(norm)
    csum[...] = jnp.zeros_like(csum)
    for move in tables:
        move.wait()
    for s in range(subs):
        for move in fetch(s):
            move.wait()
        for f in range(faces):
            rows = load[s, f * block : (f + 1) * block, :]
            norm[...] += fold_rows(rows * rows)
            if copies and (f >= half and s < subs // 2):
                continue
            trace = jnp.dot(mortar[s, f], rows.astype(BF16), preferred_element_type=F32).astype(BF16)
            if f < half:
                up[partner[s, f]] = trace
            else:
                low[(s - subs // 2 if copies else s) * half + f - half] = trace
        for c in range(corners):
            row = pl.ds(cmap[s, c], 1)
            csum[row, :] += load[s, c * stride : c * stride + 1, :]


def stiff_product(schur_hbm, mortar, *refs):
    loads, (out_a, out_b, schur, flipped, sems) = refs[:-5], refs[-5:]
    subs = schur.shape[0]

    def fetch(s):
        return pltpu.make_async_copy(schur_hbm.at[s], schur.at[s], sems.at[s])

    for s in range(subs):
        fetch(s).start()

    def work(s, _):
        fetch(s).wait()
        value = jnp.concatenate([load[s].astype(BF16) for load in loads], axis=1)
        product = jnp.dot(schur[s], value, preferred_element_type=F32)
        out_a[s] = product[:, : out_a.shape[2]]
        out_b[s] = product[:, out_a.shape[2] :]
        for f in range(mortar.shape[1]):
            flipped[s, f] = mortar[s, f].T
        return 0

    lax.fori_loop(0, subs, work, 0)


def first_image(lo, pieces, groups, share, partner_hbm, cmap_hbm, mortar, flipped, stiff, csum, cinv, *refs):
    ins, earlier, refs = refs[: 6 * pieces], refs[6 * pieces], refs[6 * pieces + 1 :]
    loads, norms, ups, lows, aboves, belows = (ins[i * pieces : (i + 1) * pieces] for i in range(6))
    refs, joined = refs[:-2], refs[-2:]
    tail_in, (send, rest), refs = refs[:-11], refs[-10:-8], refs[-11:-10] + refs[-8:]
    image, low_out, jump_out, sums, cval, up_out, partner, cmap, sems = refs
    subs, order, width = image.shape
    faces, block = mortar.shape[1], mortar.shape[2]
    half = faces // 2
    corners = cmap.shape[1]
    coarse = csum.shape[0]
    stride = order // corners
    cols = slice(lo, lo + width)
    if not lo:
        for whole, start, more in zip(joined, (lows[0], aboves[0]), tail_in):
            whole[: start.shape[0]] = start[...]
            whole[start.shape[0] :] = more[...]
        lows, aboves = joined[:1] + lows[1:], joined[1:] + aboves[1:]
    tables = fetch_tables(partner_hbm, cmap_hbm, partner, cmap, sems)
    for move in tables:
        move.start()
    sums[...] = jnp.zeros_like(sums)
    cval[...] = jnp.dot(cinv[0], csum[:, cols], precision=lax.Precision.HIGHEST, preferred_element_type=F32)
    for move in tables:
        move.wait()

    def difference(own, other, slot):
        return jnp.concatenate(
            [(a[slot].astype(F32) - b[slot].astype(F32)).astype(BF16) for a, b in zip(own, other)], axis=1
        )

    def work(s, curv):
        for f in range(faces):
            if f < half:
                jump = difference(ups, aboves, partner[s, f])
            else:
                jump = difference(lows, belows, s * half + f - half)
                jump_out[s * half + f - half] = jump
            pulled = jnp.dot(flipped[s, f], jump, preferred_element_type=F32)
            rows = slice(f * block, (f + 1) * block)
            image[s, rows, :] = stiff[s, rows, :] + pulled
        for c in range(corners):
            row = pl.ds(cmap[s, c], 1)
            at = slice(c * stride, c * stride + 1)
            value = image[s, at, :] + cval[row, :]
            image[s, at, :] = value
            sums[row, :] += value
        for f in range(faces):
            at = slice(f * block, (f + 1) * block)
            rows = image[s, at, :]
            curv = tuple(
                acc + fold_rows(load[s, at, :] * rows[:, group_cols(j)])
                for j, (acc, load) in enumerate(zip(curv, loads))
            )
            trace = jnp.dot(mortar[s, f], rows.astype(BF16), preferred_element_type=F32).astype(BF16)
            if f < half:
                up_out[partner[s, f]] = trace
            else:
                low_out[s * half + f - half] = trace
        return curv

    curv = lax.fori_loop(0, subs, work, tuple(jnp.zeros((8, LANES), F32) for _ in loads))
    first = lo // LANES
    if first:
        kept = first * tail_in[0].shape[0]
        for at in range(kept):
            send[at] = tail_in[0][at // first, :, group_cols(at % first)]
        send[kept:] = up_out[: send.shape[0] - kept]
    else:
        send[...] = up_out[: send.shape[0]]
    rest[...] = up_out[up_out.shape[0] - rest.shape[0] :]
    for j in range(pieces):
        for row, value in ((first + j, norms[j][...]), (groups + first + j, curv[j])):
            sums[coarse + row : coarse + row + 1, :LANES] = row_sum(value)
    for j in range(first):
        for row in (j, groups + j):
            at = slice(coarse + row, coarse + row + 1)
            sums[at, :] = share * earlier[at, :LANES]


def residual_sums(share, hops, groups, *refs):
    parts, refs = refs[:hops], refs[hops:]
    schur, csum, cinv, csum_a, csum_b, image_a, image_b = refs[:7]
    loads, (low, jump), refs = refs[7 : 7 + groups], refs[7 + groups : 9 + groups], refs[9 + groups :]
    recvs, (total, norm, energy, resid) = refs[:-4], refs[-4:]
    coarse = csum.shape[0]
    value = jnp.where(lax.axis_index("sub") + 1 >= hops, parts[0][...], 0.0)
    for ref in parts[1:]:
        value += ref[...]
    for j in range(groups):
        total[0:1, group_cols(j)] = value[j : j + 1, :]
        total[1:2, group_cols(j)] = value[groups + j : groups + j + 1, :]
    step = total[0:1, :] / total[1:2, :]
    inner = jnp.concatenate([csum_a[:coarse, :], csum_b[:coarse, :]], axis=1)
    change = csum[...] - step * inner
    field = jnp.dot(cinv[0], change, precision=lax.Precision.HIGHEST, preferred_element_type=F32)
    norm[...] = jnp.zeros_like(norm)
    energy[...] = share * fold_rows(change * field)

    slots, subs, order = low.shape[0], schur.shape[0], schur.shape[1]
    tile = min(256, order)

    def received(k, j):
        whole, mixed = recvs
        if k < whole.shape[0]:
            return whole[k, :, group_cols(j)]
        return mixed[(k - whole.shape[0]) * (groups - 1) + j]

    for s in range(subs):
        for j, load in enumerate(loads):
            cols = group_cols(j)
            image, own = (image_a, cols) if j + 1 < groups else (image_b, group_cols(0))
            resid[:, cols] = load[s] - step[:, cols] * image[s, :, own]
        r = resid[...]
        norm[...] += fold_rows(r * r)
        half = r.astype(BF16)
        for i in range(0, order, tile):
            rows = slice(i, i + tile)
            beyond = half[rows, :]
            if i + tile < order:
                beyond = jnp.concatenate([beyond, half[i + tile :, :] * BF16(2.0)], axis=0)
            product = jnp.dot(schur[s, rows, i:], beyond, preferred_element_type=F32)
            energy[...] += fold_rows(r[rows, :] * product)
        for j in range(groups - 1):
            cols = group_cols(j)
            acc = energy[:, cols]
            for k in range(s * slots // subs, (s + 1) * slots // subs):
                delta = low[k, :, cols].astype(F32) - received(k, j).astype(F32)
                value = jump[k, :, cols].astype(F32) - step[:, cols] * delta
                acc += fold_rows(value * value)
            energy[:, cols] = acc


def jump_squares(step, low, jump, recvs, cols):
    acc, start = jnp.zeros((8, LANES), F32), low.shape[0] - sum(recv.shape[0] for recv in recvs)
    for recv in recvs:

        def one(k, acc, recv=recv, start=start):
            delta = low[start + k, :, cols].astype(F32) - recv[k, :, cols].astype(F32)
            value = jump[start + k, :, cols].astype(F32) - step * delta
            return acc + fold_rows(value * value)

        acc = lax.fori_loop(max(-start, 0), recv.shape[0], one, acc, unroll=True)
        start += recv.shape[0]
    return acc


def last_sums(total, norm, energy, low, jump, *refs):
    recvs, out = refs[:-1], refs[-1]
    groups = norm.shape[1] // LANES
    last = group_cols(groups - 1)
    step = total[0:1, last] / total[1:2, last]
    ending = row_sum(energy[:, last] + jump_squares(step, low, jump, recvs, group_cols(0)))
    sums = jnp.concatenate([row_sum(energy[:, : last.start]), ending], axis=1)
    rows = jnp.concatenate([row_sum(norm[...]), sums], axis=0)
    for d in range(out.shape[0]):
        out[d] = rows


def finish(total, gathered, *refs):
    loads, (image_a, image_b, out_hbm, stage, sems) = refs[:-5], refs[-5:]
    groups = len(loads)
    subs = stage.shape[0]
    second = jnp.sum(gathered[...], axis=0)

    pieces = sems.shape[1]
    size = stage.shape[1] // pieces

    def send(s, p):
        rows = pl.ds(p * size, size)
        return pltpu.make_async_copy(stage.at[s, rows], out_hbm.at[s, rows], sems.at[s, p])

    scales = []
    for j in range(groups):
        norm0 = total[0:1, group_cols(j)]
        step = norm0 / total[1:2, group_cols(j)]
        norm1 = second[0:1, group_cols(j)]
        beta = norm1 / norm0
        step2 = norm1 / (second[1:2, group_cols(j)] - beta * norm1 / step)
        scales.append((step + step2 * (1.0 + beta), step2 * step))
    for s in range(subs):
        for p in range(pieces):
            rows = slice(p * size, (p + 1) * size)
            for j in range(groups):
                image, cols = (image_a, group_cols(j)) if j + 1 < groups else (image_b, group_cols(0))
                stage[s, rows, group_cols(j)] = scales[j][0] * loads[j][s, rows] - scales[j][1] * image[s, rows, cols]
            send(s, p).start()
    for s in range(subs):
        for p in range(pieces):
            send(s, p).wait()


def call(kernel, in_specs, outs, scratch=(), limit=5, in_hbm=(), alias=None):
    return pl.pallas_call(
        kernel,
        in_specs=in_specs,
        out_specs=[ANY if i in in_hbm else VMEM for i in range(len(outs))],
        out_shape=outs,
        scratch_shapes=list(scratch),
        input_output_aliases=alias or {},
        compiler_params=pltpu.CompilerParams(vmem_limit_bytes=limit * 2**20),
    )


def iterate(schur, mortar, partner, corner_map, coarse_inv, load):
    subs, order, columns = load.shape
    faces, block = mortar.shape[1], mortar.shape[2]
    half = faces // 2
    slots = subs * half
    coarse = coarse_inv.shape[1]
    groups = columns // LANES
    dma = pltpu.SemaphoreType.DMA
    table_scratch = [pltpu.SMEM(partner.shape, partner.dtype), pltpu.SMEM(corner_map.shape, corner_map.dtype)]
    tables = (hbm(partner), hbm(corner_map))

    def traces_of(width):
        return pltpu.VMEM((slots, block, width), BF16)

    loads, norms, ups, lows, csums, aboves, belows = [], [], [], [], [], [], []
    half_traces = pltpu.VMEM((slots // 2, block, LANES), BF16)
    held_mortar = hbm(mortar)
    lead = call(
        lead_traces, [ANY, ANY], [half_traces],
        [pltpu.VMEM((subs // 2, half * block, LANES), F32),
         pltpu.VMEM((subs // 2, half, block, block), BF16), dma((2, subs))],
    )(hbm(load), held_mortar)[0]
    aboves.append(vmem(shifted(lead, "sub", -1)))
    for j in range(groups):
        outs = [pltpu.VMEM((subs, order, LANES), F32)]
        if j == 0:
            outs.append(pltpu.VMEM(mortar.shape, BF16))
        outs += [traces_of(LANES), traces_of(LANES) if j else half_traces] + [pltpu.VMEM((8, LANES), F32), pltpu.VMEM((coarse, LANES), F32)]
        got = list(call(
            functools.partial(first_traces, j * LANES, j == 0),
            [ANY, ANY, ANY, ANY if j == 0 else VMEM], outs, table_scratch + [dma((3, max(subs, 2)))],
        )(*tables, hbm(load), held_mortar))
        loads.append(vmem(got.pop(0)))
        if j == 0:
            held_mortar = vmem(got.pop(0))
        above = vmem(shifted(got[1], "sub", -1))
        belows.append(vmem(shifted(got[0], "sub", 1)))
        if j:
            aboves.append(above)
        else:
            others, got[1] = [vmem(got[1]), above], lead
        ups.append(vmem(got[0]))
        lows.append(vmem(got[1]))
        norms.append(vmem(got[2]))
        csums.append(got[3])
    csum = vmem(group_sum(jnp.concatenate(csums, axis=1), "grp"))

    *stiff, held_schur, flipped = call(
        stiff_product, [ANY] + [VMEM] * (1 + groups),
        [pltpu.VMEM((subs, order, w), F32) for w in (columns - LANES, LANES)]
        + [pltpu.VMEM(schur.shape, BF16), pltpu.VMEM(mortar.shape, BF16)], [dma((subs,))],
    )(hbm(schur), held_mortar, *loads)
    held_schur, flipped = vmem(held_schur), vmem(flipped)

    bounds = ((0, groups - 1), (groups - 1, groups))
    share = 1.0 / lax.axis_size("grp")
    images, jumps, low2s, recvs, csum2s, tails = [], [], [], [], [], []
    tail, lead_slots = slots // 16, 7 * slots // 16
    cuts = ((slots - tail, tail), ((groups - 1) * tail + lead_slots, slots - lead_slots))
    for k, (lo, hi) in enumerate(bounds):
        n, w = hi - lo, (hi - lo) * LANES
        pick = [x[lo:hi] for x in (loads, norms, ups, lows, aboves, belows)]
        got = call(
            functools.partial(first_image, lo * LANES, n, groups, share),
            [ANY, ANY] + [VMEM] * (8 + 6 * n - k),
            [pltpu.VMEM((subs, order, w), F32)]
            + [pltpu.VMEM((size, block, w), BF16) for size in cuts[k]]
            + [traces_of(w)] * 2 + [pltpu.VMEM((coarse + 8, w), F32)],
            [pltpu.VMEM((coarse, w), F32), traces_of(w)] + table_scratch + [dma((2,))]
            + [traces_of(LANES)] * 2, alias={4: 0},
        )(*tables, held_mortar, flipped, vmem(stiff[k]), csum, coarse_inv, *sum(pick, []), csum2s[0] if k else csum, *(tails if k else others))
        image, *up2, low2, jump, sums = got
        images.append(vmem(image))
        low2s.append(vmem(low2))
        jumps.append(vmem(jump))
        sums = group_sum(sums, "grp")
        if not k:
            csum, sums = lax.optimization_barrier((csum, sums))
            csum = vmem(csum)
        csum2s.append(vmem(sums))
        held = up2.pop() if not k else None
        tails = [vmem(held)] if not k else []
        for piece in up2:
            recvs.append(vmem(shifted(piece, "sub", 1)))

    totals = [vmem(x) for x in hub_sum(sums[coarse:], "sub")]
    hops = len(totals)
    total, norm1, energy = call(
        functools.partial(residual_sums, share, hops, groups),
        [VMEM] * (hops + 11 + groups), [pltpu.VMEM((8, columns), F32)] * 3, [pltpu.VMEM((order, columns), F32)],
    )(*totals, held_schur, csum, coarse_inv, *csum2s, *images, *loads, low2s[0], jumps[0], *recvs[:2])
    total, norm1, energy = vmem(total), vmem(norm1), vmem(energy)

    devices = lax.axis_size("sub") * lax.axis_size("grp")
    spread = call(
        last_sums, [VMEM] * 7, [pltpu.VMEM((devices, 2, columns), F32)],
    )(total, norm1, energy, low2s[1], jumps[1], *recvs[1:])[0]
    gathered = lax.all_to_all(spread, ("sub", "grp"), 0, 0, tiled=True)

    return call(
        finish, [VMEM] * (4 + groups),
        [jax.ShapeDtypeStruct((subs, order, columns), F32)],
        [pltpu.VMEM((subs, order, columns), F32), dma((subs, 2))], limit=9, in_hbm=(0,),
    )(total, vmem(gathered), *loads, *images)[0]


def solution(mesh):
    return jax.shard_map(
        iterate,
        mesh=mesh,
        in_specs=(
            P(("sub", "grp"), None, None),
            P(("sub", "grp"), None, None, None),
            P(("sub", "grp"), None),
            P(("sub", "grp"), None),
            P("sub", None, None),
            P(("sub", "grp"), None, None),
        ),
        out_specs=P(("sub", "grp"), None, None),
        check_vma=False,
    )
```
